512 devices in a mesh: vec: 32 (over y_lo, x, core), row: 16 (over y_hi, z).
Axes of the slice: x: 4, y: 8 (y_hi: 2, y_lo: 4; y = y_hi * 4 + y_lo), z: 8, core: 2. Of those that a mesh axis runs over, the one named last changes fastest.
Arguments:
- diag_blocks: float32 [128, 256, 256], P('row'), may hold values from -0.475 to 0.475, as said below
- coupling: float32 [128, 256, 256], P('row'), may hold values from -0.078125 to 0.078125
- vectors: float32 [1024, 32768], P('vec', 'row'), may hold values from -3600 to 3600
Outputs:
- filtered: float32 [1024, 32768], P('vec', 'row')
The draws below stay inside these ranges and needn't reach their ends.
Inputs may be any that keep to these rules, and one draw needn't show every extreme that they name: `diag_blocks`: each block is symmetric.
All inputs are finite; a program needn't handle non-finite values.
Results may differ from the reference program's by a relative error of at most 0.0001.
Values sent between devices are 32-bit elements; how exact they have to be, the bound alone decides.
No kernel may reach another device: no remote copies, remote signals or barrier semaphores. Data moves between devices by JAX's collectives and lax.ppermute only.
A program may use at most 64 MiB of HBM per device.

```python
import math
import jax
import jax.numpy as jnp
from jax import lax

BLK = 256
NVEC = 1024
DEGREE = 4
NB_ALL = 128
ROWS = 32768


def draw_diag_blocks(key, part):
    key_body = jax.random.fold_in(key, 11)
    key_onsite = jax.random.fold_in(key, 12)
    block_shape = (NB_ALL, BLK, BLK)
    raw_values = jnp.clip(jax.random.normal(key_body, block_shape, jnp.float32), -4.0, 4.0)
    symmetric = (raw_values + jnp.swapaxes(raw_values, 1, 2)) * (0.2 / jnp.sqrt(2.0 * BLK))
    onsite = jax.random.uniform(key_onsite, (NB_ALL, BLK), jnp.float32, -0.4, 0.4)
    return symmetric + onsite[:, :, None] * jnp.eye(BLK, dtype=jnp.float32)[None]


def draw_vectors(key, part):
    key_base = jax.random.fold_in(key, 21)
    key_column = jax.random.fold_in(key, 22)
    key_rowscale = jax.random.fold_in(key, 23)
    column_scale = jnp.exp(jax.random.uniform(key_column, (NVEC, 1), jnp.float32, 0.0, math.log(10.0)))
    row_scale = jnp.exp(jax.random.uniform(key_rowscale, (1, ROWS), jnp.float32, 0.0, math.log(10.0)))
    position = jnp.arange(ROWS, dtype=jnp.float32)[None, :] / ROWS
    base_values = jnp.clip(jax.random.normal(key_base, (NVEC, ROWS), jnp.float32), -4.0, 4.0)
    trend = jnp.exp(math.log(3.0) * position)
    return base_values * column_scale * row_scale * trend


def level_of(key, extent, cuts, least, largest):
    factor_of, own = 1.0, jax.random.fold_in(key, 6)
    for axis_at, shards_of in cuts:
        steps = jnp.exp(jax.random.uniform(jax.random.fold_in(own, axis_at), (shards_of,), jnp.float32, least / len(cuts), largest / len(cuts)))
        factor_of = factor_of * jnp.repeat(steps, extent[axis_at] // shards_of).reshape([-1 if axis == axis_at else 1 for axis in range(len(extent))])
    return factor_of


def gaussian(key, extent, width, most, split=(), held_as=jnp.bfloat16):
    entries = width * jax.random.normal(key, extent, jnp.float32)
    if split:
        entries = entries * level_of(key, extent, split, -0.22, 0.18)
    return jnp.clip(entries, -most, most).astype(held_as)


def setup_inputs(seed: int = 0) -> dict:
    key_list = jax.random.split(jax.random.key(seed), 4)
    diag_blocks = draw_diag_blocks(jax.random.fold_in(key_list[3], 71), 0)
    coupling = gaussian(key_list[1], (NB_ALL, BLK, BLK), (0.2 * BLK ** -0.5), 0.078125, ((0, 16),), jnp.float32)
    vectors = draw_vectors(jax.random.fold_in(key_list[3], 71), 0)
    return dict(diag_blocks=diag_blocks, coupling=coupling, vectors=vectors)


filter_center = 0.1
filter_half = 1.0
epsilon = 1e-06
highest = lax.Precision.HIGHEST

def hamiltonian(field, diag_blocks, coupling):
    count_rows = field.shape[0]
    blocks = field.reshape(count_rows, NB_ALL, BLK)
    zero_block = jnp.zeros((count_rows, 1, BLK), jnp.float32)
    upper_next = jnp.concatenate([blocks[:, 1:], zero_block], axis=1)
    lower_prev = jnp.concatenate([zero_block, blocks[:, :-1]], axis=1)
    coupling_prev = jnp.concatenate([jnp.zeros((1, BLK, BLK), jnp.float32), coupling[:-1]], axis=0)
    result = jnp.einsum('vnk,njk->vnj', blocks, diag_blocks, precision=highest)
    result = result + jnp.einsum('vnk,njk->vnj', upper_next, coupling, precision=highest)
    result = result + jnp.einsum('vnk,nkj->vnj', lower_prev, coupling_prev, precision=highest)
    return result.reshape(field.shape)

def scaled_apply(field, diag_blocks, coupling):
    return (hamiltonian(field, diag_blocks, coupling) - filter_center * field) / filter_half

def reference(diag_blocks, coupling, vectors):
    previous = vectors
    current = scaled_apply(vectors, diag_blocks, coupling)
    for turn_index in range(DEGREE - 1):
        following = 2.0 * scaled_apply(current, diag_blocks, coupling) - previous
        previous = current
        current = following
    gram_sum = lax.dot_general(current, current, (((1,), (1,)), ((), ())), precision=highest)
    scales = 1.0 / jnp.sqrt(jnp.diagonal(gram_sum) / ROWS + epsilon)
    normalized = gram_sum * scales[:, None] * scales[None, :] / ROWS
    mixing = (1.5 * jnp.eye(NVEC, dtype=jnp.float32) - 0.5 * normalized) * scales[None, :]
    return jnp.dot(mixing, current, precision=highest)
```

```python
import jax
import jax.numpy as jnp
from jax import lax
from jax.sharding import Mesh, PartitionSpec as P

DEGREE = 4

filter_center = 0.1
filter_half = 1.0
epsilon = 1e-06
precision = lax.Precision.HIGH

SPLIT = (("yl", 4), ("x", 4), ("c", 2), ("yh", 2), ("z", 8))
VEC = ("yl", "x", "c")
ROW = ("yh", "z")
SUM = ("yl", "yh", "z")


def dot(a, b, contract, batch=((), ())):
    return lax.dot_general(a, b, (contract, batch), precision=precision)


def local_terms(y, diag_blocks, coupling):
    batch = ((0,), (0,))
    result = dot(y, diag_blocks, ((2,), (2,)), batch) - filter_center * y
    upper = dot(y[1:], coupling[:-1], ((2,), (2,)), batch)
    lower = dot(y[:-1], coupling[:-1], ((2,), (1,)), batch)
    none = jnp.zeros_like(y[:1])
    return result + jnp.concatenate([upper, none]) + jnp.concatenate([none, lower])


def chebyshev(vectors, diag_blocks, coupling):
    count = vectors.shape[0]
    blocks, size = diag_blocks.shape[0], diag_blocks.shape[1]
    rows = lax.axis_size(ROW)
    forward = [(i, i + 1) for i in range(rows - 1)]
    backward = [(target, source) for source, target in forward]
    y = vectors.reshape(count, blocks, size).transpose(1, 0, 2)
    last_coupling = coupling[-1]
    first, last = y[0], y[-1]
    previous = None
    for turn in range(DEGREE):
        from_above = lax.ppermute(first, ROW, backward)
        last_term = dot(last, last_coupling, ((1,), (0,)))
        from_below = lax.ppermute(last_term, ROW, forward)
        scale = (1.0 if turn == 0 else 2.0) / filter_half
        inner = scale * local_terms(y, diag_blocks, coupling)
        if previous is not None:
            inner = inner - previous
        last = inner[-1] + scale * dot(from_above, last_coupling, ((1,), (1,)))
        first = inner[0] + scale * from_below
        previous = y
        y = jnp.concatenate([first[None], inner[1:-1], last[None]])
    return y


def local(diag_blocks, coupling, vectors):
    count = vectors.shape[0]
    y = chebyshev(vectors, diag_blocks, coupling)
    blocks, _, size = y.shape
    nyl, nx, nc = (lax.axis_size(a) for a in VEC)
    total_rows = blocks * size * lax.axis_size(ROW)
    swapped = lax.all_to_all(y, "yl", split_axis=0, concat_axis=0, tiled=True)
    part = blocks // nyl
    own = swapped.reshape(nyl, part, count, size).transpose(0, 2, 1, 3)
    own = own.reshape(nyl * count, part * size)
    group, depth = own.shape
    copies = jnp.broadcast_to(own[None], (nx, group, depth))
    near = lax.all_to_all(copies, "x", split_axis=0, concat_axis=0, tiled=True)
    near = near.reshape(nx * group, depth)
    far = lax.ppermute(near, "c", [(0, 1), (1, 0)])
    half = nx * group
    members = lax.axis_size(SUM)
    gram_near = dot(own, near, ((1,), (1,)))
    gram_far = dot(own, far, ((1,), (1,)))
    squares = jnp.concatenate([jnp.sum(near * near, axis=1), jnp.sum(far * far, axis=1)])
    lanes = 2 * half // 8
    payload = jnp.concatenate(
        [
            gram_near.reshape(members, -1),
            gram_far.reshape(members, -1),
            jnp.tile(squares.reshape(8, lanes), (members // 8, 1)),
        ],
        axis=1,
    )
    pieces = lax.all_to_all(payload, SUM, split_axis=0, concat_axis=0, tiled=True)
    piece = jnp.sum(pieces, axis=0)
    spread = jnp.broadcast_to(piece[None], pieces.shape)
    summed = lax.all_to_all(spread, SUM, split_axis=0, concat_axis=0, tiled=True)
    width = group // members * half
    gram_near = summed[:, :width].reshape(group, half)
    gram_far = summed[:, width : 2 * width].reshape(group, half)
    scales = 1.0 / jnp.sqrt(summed[:8, 2 * width :].reshape(2 * half) / total_rows + epsilon)
    scales_near, scales_far = scales[:half], scales[half:]
    at = lax.axis_index("x") * group
    mine = lax.dynamic_slice(scales_near, (at,), (group,))
    same = lax.broadcasted_iota(jnp.int32, (group, half), 1) == (
        lax.broadcasted_iota(jnp.int32, (group, half), 0) + at
    )
    delta = jnp.where(same, 1.5, 0.0)
    mixing_near = (
        delta - (0.5 / total_rows) * (gram_near * mine[:, None] * scales_near[None, :])
    ) * scales_near[None, :]
    mixing_far = (
        (-0.5 / total_rows) * (gram_far * mine[:, None] * scales_far[None, :])
    ) * scales_far[None, :]
    renewed = dot(mixing_near, near, ((1,), (0,))) + dot(mixing_far, far, ((1,), (0,)))
    return lax.all_to_all(renewed, "yl", split_axis=0, concat_axis=1, tiled=True)


def solution(mesh):
    sizes = tuple(size for _, size in SPLIT)
    fine = Mesh(mesh.devices.reshape(sizes), tuple(name for name, _ in SPLIT))
    placed = (P(ROW, None, None), P(ROW, None, None), P(VEC, ROW))
    return jax.shard_map(
        local, mesh=fine, in_specs=placed, out_specs=P(VEC, ROW), check_vma=False
    )
```

```python
import functools

import jax
import jax.numpy as jnp
from jax import lax
from jax.experimental import pallas as pl
from jax.experimental.pallas import tpu as pltpu
from jax.sharding import Mesh, PartitionSpec as P

DEGREE = 4

filter_center = 0.1
filter_half = 1.0
epsilon = 1e-06
precision = lax.Precision.HIGH

SPLIT = (("yl", 4), ("x", 4), ("c", 2), ("yh", 2), ("z", 8))
VEC = ("yl", "x", "c")
ROW = ("yh", "z")
SUM = ("yl", "yh", "z")

TILE, LANES = 8, 128
INTERPRET = False


def dot(a, b, contract, batch=((), ())):
    return lax.dot_general(a, b, (contract, batch), precision=precision)


def local_terms(y, diag_blocks, coupling):
    batch = ((0,), (0,))
    result = dot(y, diag_blocks, ((2,), (2,)), batch) - filter_center * y
    upper = dot(y[1:], coupling[:-1], ((2,), (2,)), batch)
    lower = dot(y[:-1], coupling[:-1], ((2,), (1,)), batch)
    none = jnp.zeros_like(y[:1])
    return result + jnp.concatenate([upper, none]) + jnp.concatenate([none, lower])


def chebyshev(vectors, diag_blocks, coupling):
    count = vectors.shape[0]
    blocks, size = diag_blocks.shape[0], diag_blocks.shape[1]
    rows = lax.axis_size(ROW)
    forward = [(i, i + 1) for i in range(rows - 1)]
    backward = [(target, source) for source, target in forward]
    y = vectors.reshape(count, blocks, size).transpose(1, 0, 2)
    last_coupling = coupling[-1]
    first, last = y[0], y[-1]
    previous = None
    for turn in range(DEGREE):
        from_above = lax.ppermute(first, ROW, backward)
        last_term = dot(last, last_coupling, ((1,), (0,)))
        from_below = lax.ppermute(last_term, ROW, forward)
        scale = (1.0 if turn == 0 else 2.0) / filter_half
        inner = scale * local_terms(y, diag_blocks, coupling)
        if previous is not None:
            inner = inner - previous
        last = inner[-1] + scale * dot(from_above, last_coupling, ((1,), (1,)))
        first = inner[0] + scale * from_below
        previous = y
        y = jnp.concatenate([first[None], inner[1:-1], last[None]])
    return y


def split(a):
    high = a.astype(jnp.bfloat16)
    return high, (a - high.astype(jnp.float32)).astype(jnp.bfloat16)


def product(a, b, contract):
    def one(x, y):
        return lax.dot_general(x, y, (contract, ((), ())), preferred_element_type=jnp.float32)

    return one(a[0], b[0]) + (one(a[0], b[1]) + one(a[1], b[0]))


def gram_kernel(own_ref, near_ref, far_ref, out_ref):
    own = split(own_ref[...])
    ones = jnp.ones((TILE, own_ref.shape[1]), jnp.bfloat16)
    tiles, squares = [], []
    for ref in (near_ref, far_ref):
        tiles.append(product(own, split(ref[...]), ((1,), (1,))))
        square = split(ref[...] * ref[...])
        sums = [
            lax.dot_general(ones, part, (((1,), (1,)), ((), ())), preferred_element_type=jnp.float32)
            for part in square
        ]
        squares.append(sums[0] + sums[1])
    across = near_ref.shape[0] // LANES
    step = 2 * TILE + 1
    for m in range(out_ref.shape[0] // step):
        i, j = m // across * TILE, m % across * LANES
        for side in range(2):
            out_ref[step * m + TILE * side : step * m + TILE * (side + 1), :] = tiles[side][
                i : i + TILE, j : j + LANES
            ]
        side, j = m % (2 * across) // across, m % across * LANES
        out_ref[step * m + 2 * TILE : step * (m + 1), :] = squares[side][:1, j : j + LANES]


def sum_kernel(in_ref, out_ref):
    step = 2 * TILE + 1
    group = TILE * step
    count = in_ref.shape[0] // group
    total = in_ref[:group, :]
    for g in range(1, count):
        total = total + in_ref[group * g : group * (g + 1), :]
    out_ref[:group, :] = total
    piece = out_ref[:step, :]
    for m in range(1, TILE):
        piece = piece + out_ref[step * m : step * (m + 1), :]
    for m in range(TILE):
        out_ref[step * m : step * (m + 1), :] = piece
    total = out_ref[:group, :]
    for g in range(1, count):
        out_ref[group * g : group * (g + 1), :] = total


def mixing_kernel(total_rows, at_ref, summed_ref, own_ref, near_ref, far_ref, out_ref):
    step = 2 * TILE + 1
    across = near_ref.shape[0] // LANES
    group = own_ref.shape[0]

    def scales_of(m):
        row = summed_ref[pl.ds(step * m + 2 * TILE, 1), :]
        return 1.0 / jnp.sqrt(row / total_rows + epsilon)

    on_diagonal = lax.broadcasted_iota(jnp.int32, (group, LANES), 0) == (
        lax.broadcasted_iota(jnp.int32, (group, LANES), 1)
    )
    mine = jnp.sum(jnp.where(on_diagonal, scales_of(at_ref[0]), 0.0), axis=1, keepdims=True)
    result = 1.5 * mine * own_ref[...]
    for side, ref in enumerate((near_ref, far_ref)):
        columns = []
        for j in range(across):
            column = jnp.concatenate(
                [
                    summed_ref[step * m + TILE * side : step * m + TILE * (side + 1), :]
                    for m in range(j, group // TILE * across, across)
                ]
            )
            scale = scales_of(side * across + j)
            columns.append((0.5 / total_rows) * (column * mine * scale) * scale)
        mixing = jnp.concatenate(columns, axis=1)
        result = result - product(split(mixing), split(ref[...]), ((1,), (0,)))
    out_ref[...] = result


def call(kernel, out_shape, name, scalars, *arrays):
    vmem = pl.BlockSpec(memory_space=pltpu.VMEM)
    smem = pl.BlockSpec(memory_space=pltpu.SMEM)
    return pl.pallas_call(
        kernel,
        out_shape=jax.ShapeDtypeStruct(out_shape, jnp.float32),
        in_specs=[smem] * len(scalars) + [vmem] * len(arrays),
        out_specs=vmem,
        name=name,
        compiler_params=pltpu.CompilerParams(vmem_limit_bytes=24 * 2**20),
        interpret=INTERPRET,
    )(*scalars, *arrays)


def local(diag_blocks, coupling, vectors):
    count = vectors.shape[0]
    y = chebyshev(vectors, diag_blocks, coupling)
    blocks, _, size = y.shape
    nyl, nx, nc = (lax.axis_size(a) for a in VEC)
    total_rows = blocks * size * lax.axis_size(ROW)
    swapped = lax.all_to_all(y, "yl", split_axis=0, concat_axis=0, tiled=True)
    part = blocks // nyl
    own = swapped.reshape(nyl, part, count, size).transpose(0, 2, 1, 3)
    own = own.reshape(nyl * count, part * size)
    group, depth = own.shape
    copies = jnp.broadcast_to(own[None], (nx, group, depth))
    near = lax.all_to_all(copies, "x", split_axis=0, concat_axis=0, tiled=True)
    near = near.reshape(nx * group, depth)
    far = lax.ppermute(near, "c", [(0, 1), (1, 0)])
    members = group // TILE * nx
    packed = (members * (2 * TILE + 1), LANES)

    def exchange(a):
        a = a.reshape(lax.axis_size(SUM), -1)
        return lax.all_to_all(a, SUM, split_axis=0, concat_axis=0, tiled=True).reshape(packed)

    pieces = exchange(call(gram_kernel, packed, "gram", (), own, near, far))
    summed = exchange(call(sum_kernel, packed, "sum", (), pieces))
    renewed = call(
        functools.partial(mixing_kernel, total_rows),
        (group, depth),
        "mixing",
        (lax.axis_index("x").reshape(1),),
        summed,
        own,
        near,
        far,
    )
    return lax.all_to_all(renewed, "yl", split_axis=0, concat_axis=1, tiled=True)


def solution(mesh):
    sizes = tuple(size for _, size in SPLIT)
    fine = Mesh(mesh.devices.reshape(sizes), tuple(name for name, _ in SPLIT))
    placed = (P(ROW, None, None), P(ROW, None, None), P(VEC, ROW))
    return jax.shard_map(
        local, mesh=fine, in_specs=placed, out_specs=P(VEC, ROW), check_vma=False
    )
```

```python
import functools

import jax
import jax.numpy as jnp
from jax import lax
from jax.experimental import pallas as pl
from jax.experimental.pallas import tpu as pltpu
from jax.sharding import Mesh, PartitionSpec as P


DEGREE = 4

filter_center = 0.1
filter_half = 1.0
epsilon = 1e-06
precision = lax.Precision.HIGH

SPLIT = (("yl", 4), ("x", 4), ("c", 2), ("yh", 2), ("z", 8))
VEC = ("yl", "x", "c")
ROW = ("yh", "z")
SUM = ("yl", "yh", "z")

TILE, LANES = 8, 128
INTERPRET = False


def dot(a, b, contract, batch=((), ())):
    return lax.dot_general(a, b, (contract, batch), precision=precision)


def local_terms(y, diag_blocks, coupling):
    batch = ((0,), (0,))
    result = dot(y, diag_blocks, ((2,), (2,)), batch) - filter_center * y
    upper = dot(y[1:], coupling[:-1], ((2,), (2,)), batch)
    lower = dot(y[:-1], coupling[:-1], ((2,), (1,)), batch)
    none = jnp.zeros_like(y[:1])
    return result + jnp.concatenate([upper, none]) + jnp.concatenate([none, lower])


def chebyshev(vectors, diag_blocks, coupling):
    count = vectors.shape[0]
    blocks, size = diag_blocks.shape[0], diag_blocks.shape[1]
    rows = lax.axis_size(ROW)
    swaps = []
    for start in (1, 0):
        ups = [(i, i + 1) for i in range(start, rows - 1, 2)]
        swaps.append(ups + [(above, below) for below, above in ups])
    is_odd = lax.axis_index(ROW) % 2 == 1
    y = vectors.reshape(count, blocks, size).transpose(1, 0, 2)
    last_coupling = coupling[-1]
    first, last = y[0], y[-1]
    previous = None
    for turn in range(DEGREE):
        last_term = dot(last, last_coupling, ((1,), (0,)))
        odd = lax.ppermute(jnp.where(is_odd, last_term, first), ROW, swaps[0])
        even = lax.ppermute(jnp.where(is_odd, first, last_term), ROW, swaps[1])
        scale = (1.0 if turn == 0 else 2.0) / filter_half
        inner = scale * local_terms(y, diag_blocks, coupling)
        if previous is not None:
            inner = inner - previous
        from_above = jnp.where(is_odd, odd, even)
        from_below = jnp.where(is_odd, even, odd)
        last = inner[-1] + scale * dot(from_above, last_coupling, ((1,), (1,)))
        first = inner[0] + scale * from_below
        previous = y
        y = jnp.concatenate([first[None], inner[1:-1], last[None]])
    return y


def split(a):
    high = a.astype(jnp.bfloat16)
    return high, (a - high.astype(jnp.float32)).astype(jnp.bfloat16)


def product(a, b, contract):
    def one(x, y):
        return lax.dot_general(x, y, (contract, ((), ())), preferred_element_type=jnp.float32)

    return one(a[0], b[0]) + (one(a[0], b[1]) + one(a[1], b[0]))


def gram_kernel(own_ref, near_ref, far_ref, out_ref):
    own = split(own_ref[...])
    ones = jnp.ones((TILE, own_ref.shape[1]), jnp.bfloat16)
    tiles, squares = [], []
    for ref in (near_ref, far_ref):
        tiles.append(product(own, split(ref[...]), ((1,), (1,))))
        square = split(ref[...] * ref[...])
        sums = [
            lax.dot_general(ones, part, (((1,), (1,)), ((), ())), preferred_element_type=jnp.float32)
            for part in square
        ]
        squares.append(sums[0] + sums[1])
    across = near_ref.shape[0] // LANES
    step = 2 * TILE + 1
    for m in range(out_ref.shape[0] // step):
        i, j = m // across * TILE, m % across * LANES
        for side in range(2):
            out_ref[step * m + TILE * side : step * m + TILE * (side + 1), :] = tiles[side][
                i : i + TILE, j : j + LANES
            ]
        side, j = m % (2 * across) // across, m % across * LANES
        out_ref[step * m + 2 * TILE : step * (m + 1), :] = squares[side][:1, j : j + LANES]


def sum_kernel(in_ref, out_ref):
    step = 2 * TILE + 1
    group = TILE * step
    count = in_ref.shape[0] // group
    total = in_ref[:group, :]
    for g in range(1, count):
        total = total + in_ref[group * g : group * (g + 1), :]
    out_ref[:group, :] = total
    piece = out_ref[:step, :]
    for m in range(1, TILE):
        piece = piece + out_ref[step * m : step * (m + 1), :]
    for m in range(TILE):
        out_ref[step * m : step * (m + 1), :] = piece
    total = out_ref[:group, :]
    for g in range(1, count):
        out_ref[group * g : group * (g + 1), :] = total


def mixing_kernel(total_rows, at_ref, summed_ref, own_ref, near_ref, far_ref, out_ref):
    step = 2 * TILE + 1
    across = near_ref.shape[0] // LANES
    group = own_ref.shape[0]

    def scales_of(m):
        row = summed_ref[pl.ds(step * m + 2 * TILE, 1), :]
        return 1.0 / jnp.sqrt(row / total_rows + epsilon)

    on_diagonal = lax.broadcasted_iota(jnp.int32, (group, LANES), 0) == (
        lax.broadcasted_iota(jnp.int32, (group, LANES), 1)
    )
    mine = jnp.sum(jnp.where(on_diagonal, scales_of(at_ref[0]), 0.0), axis=1, keepdims=True)
    result = 1.5 * mine * own_ref[...]
    for side, ref in enumerate((near_ref, far_ref)):
        columns = []
        for j in range(across):
            column = jnp.concatenate(
                [
                    summed_ref[step * m + TILE * side : step * m + TILE * (side + 1), :]
                    for m in range(j, group // TILE * across, across)
                ]
            )
            scale = scales_of(side * across + j)
            columns.append((0.5 / total_rows) * (column * mine * scale) * scale)
        mixing = jnp.concatenate(columns, axis=1)
        result = result - product(split(mixing), split(ref[...]), ((1,), (0,)))
    out_ref[...] = result


def call(kernel, out_shape, scalars, *arrays):
    vmem = pl.BlockSpec(memory_space=pltpu.VMEM)
    smem = pl.BlockSpec(memory_space=pltpu.SMEM)
    return pl.pallas_call(
        kernel,
        out_shape=jax.ShapeDtypeStruct(out_shape, jnp.float32),
        in_specs=[smem] * len(scalars) + [vmem] * len(arrays),
        out_specs=vmem,
        compiler_params=pltpu.CompilerParams(vmem_limit_bytes=24 * 2**20),
        interpret=INTERPRET,
    )(*scalars, *arrays)


def local(diag_blocks, coupling, vectors):
    count = vectors.shape[0]
    at, vectors = lax.optimization_barrier((lax.axis_index("x").reshape(1), vectors))
    y = chebyshev(vectors, diag_blocks, coupling)
    blocks, _, size = y.shape
    nyl, nx, _ = (lax.axis_size(a) for a in VEC)
    total_rows = blocks * size * lax.axis_size(ROW)
    swapped = lax.all_to_all(y, "yl", split_axis=0, concat_axis=0, tiled=True)
    part = blocks // nyl
    own = swapped.reshape(nyl, part, count, size).transpose(0, 2, 1, 3)
    own = own.reshape(nyl * count, part * size)
    group, depth = own.shape
    copies = jnp.broadcast_to(own[None], (nx, group, depth))
    near = lax.all_to_all(copies, "x", split_axis=0, concat_axis=0, tiled=True)
    near = near.reshape(nx * group, depth)
    far = lax.ppermute(near, "c", [(0, 1), (1, 0)])
    members = group // TILE * nx
    packed = (members * (2 * TILE + 1), LANES)

    def exchange(a):
        a = a.reshape(lax.axis_size(SUM), -1)
        return lax.all_to_all(a, SUM, split_axis=0, concat_axis=0, tiled=True).reshape(packed)

    pieces = exchange(call(gram_kernel, packed, (), own, near, far))
    summed = exchange(call(sum_kernel, packed, (), pieces))
    renewed = call(
        functools.partial(mixing_kernel, total_rows), (group, depth), (at,), summed, own, near, far
    )
    return lax.all_to_all(renewed, "yl", split_axis=0, concat_axis=1, tiled=True)


def solution(mesh):
    sizes = tuple(size for _, size in SPLIT)
    fine = Mesh(mesh.devices.reshape(sizes), tuple(name for name, _ in SPLIT))
    placed = (P(ROW, None, None), P(ROW, None, None), P(VEC, ROW))
    return jax.shard_map(
        local, mesh=fine, in_specs=placed, out_specs=P(VEC, ROW), check_vma=False
    )
```

```python
import functools

import jax
import jax.numpy as jnp
from jax import lax
from jax.experimental import pallas as pl
from jax.experimental.pallas import tpu as pltpu
from jax.sharding import Mesh, PartitionSpec as P


DEGREE = 4

filter_center = 0.1
filter_half = 1.0
epsilon = 1e-06
precision = lax.Precision.HIGH

SPLIT = (("yl", 4), ("x", 4), ("c", 2), ("yh", 2), ("z", 8))
VEC = ("yl", "x", "c")
ROW = ("yh", "z")
SUM = ("yl", "yh", "z")

TILE, LANES = 8, 128
INTERPRET = False


def dot(a, b, contract, batch=((), ())):
    return lax.dot_general(a, b, (contract, batch), precision=precision)


def flipped(yh, z):
    return (yh + z) % 2 == 0


def snake():
    nyl, nyh, nz = (lax.axis_size(a) for a in SUM)
    places = []
    for yh in range(nyh):
        for z in range(nz):
            order = range(nyl)
            for yl in reversed(order) if flipped(yh, z) else order:
                places.append((yl * nyh + yh) * nz + z)
    return places


def local_terms(y, diag_blocks, coupling):
    terms = []
    for n, block in enumerate(y):
        term = dot(block, diag_blocks[n], ((1,), (1,))) - filter_center * block
        if n + 1 < len(y):
            term = term + dot(y[n + 1], coupling[n], ((1,), (1,)))
        if n > 0:
            term = term + dot(y[n - 1], coupling[n - 1], ((1,), (0,)))
        terms.append(term)
    return terms


def chebyshev(y, diag_blocks, coupling, is_odd):
    places = snake()
    swaps = []
    for start in (1, 0):
        ups = [(places[i], places[i + 1]) for i in range(start, len(places) - 1, 2)]
        swaps.append(ups + [(above, below) for below, above in ups])
    previous = None
    for turn in range(DEGREE):
        last_term = dot(y[-1], coupling[-1], ((1,), (0,)))
        odd = lax.ppermute(jnp.where(is_odd, last_term, y[0]), SUM, swaps[0])
        even = lax.ppermute(jnp.where(is_odd, y[0], last_term), SUM, swaps[1])
        scale = (1.0 if turn == 0 else 2.0) / filter_half
        inner = [scale * term for term in local_terms(y, diag_blocks, coupling)]
        if previous is not None:
            inner = [term - old for term, old in zip(inner, previous)]
        from_above = jnp.where(is_odd, odd, even)
        from_below = jnp.where(is_odd, even, odd)
        inner[-1] = inner[-1] + scale * dot(from_above, coupling[-1], ((1,), (1,)))
        inner[0] = inner[0] + scale * from_below
        previous, y = y, inner
    return y


def split(a):
    high = a.astype(jnp.bfloat16)
    return high, (a - high.astype(jnp.float32)).astype(jnp.bfloat16)


def product(a, b, contract):
    def one(x, y):
        return lax.dot_general(x, y, (contract, ((), ())), preferred_element_type=jnp.float32)

    return one(a[0], b[0]) + (one(a[0], b[1]) + one(a[1], b[0]))


def gram_kernel(own_ref, near_ref, far_ref, out_ref):
    own = split(own_ref[...])
    ones = jnp.ones((TILE, own_ref.shape[1]), jnp.bfloat16)
    tiles, squares = [], []
    for ref in (near_ref, far_ref):
        tiles.append(product(own, split(ref[...]), ((1,), (1,))))
        square = split(ref[...] * ref[...])
        sums = [
            lax.dot_general(ones, part, (((1,), (1,)), ((), ())), preferred_element_type=jnp.float32)
            for part in square
        ]
        squares.append(sums[0] + sums[1])
    across = near_ref.shape[0] // LANES
    step = 2 * TILE + 1
    for m in range(out_ref.shape[0] // step):
        i, j = m // across * TILE, m % across * LANES
        for side in range(2):
            out_ref[step * m + TILE * side : step * m + TILE * (side + 1), :] = tiles[side][
                i : i + TILE, j : j + LANES
            ]
        side, j = m % (2 * across) // across, m % across * LANES
        out_ref[step * m + 2 * TILE : step * (m + 1), :] = squares[side][:1, j : j + LANES]


def sum_kernel(in_ref, out_ref):
    step = 2 * TILE + 1
    group = TILE * step
    count = in_ref.shape[0] // group
    total = in_ref[:group, :]
    for g in range(1, count):
        total = total + in_ref[group * g : group * (g + 1), :]
    out_ref[:group, :] = total
    piece = out_ref[:step, :]
    for m in range(1, TILE):
        piece = piece + out_ref[step * m : step * (m + 1), :]
    for m in range(TILE):
        out_ref[step * m : step * (m + 1), :] = piece
    total = out_ref[:group, :]
    for g in range(1, count):
        out_ref[group * g : group * (g + 1), :] = total


def mixing_kernel(total_rows, at_ref, summed_ref, own_ref, near_ref, far_ref, out_ref):
    step = 2 * TILE + 1
    across = near_ref.shape[0] // LANES
    group = own_ref.shape[0]

    def scales_of(m):
        row = summed_ref[pl.ds(step * m + 2 * TILE, 1), :]
        return 1.0 / jnp.sqrt(row / total_rows + epsilon)

    on_diagonal = lax.broadcasted_iota(jnp.int32, (group, LANES), 0) == (
        lax.broadcasted_iota(jnp.int32, (group, LANES), 1)
    )
    mine = jnp.sum(jnp.where(on_diagonal, scales_of(at_ref[0]), 0.0), axis=1, keepdims=True)
    result = 1.5 * mine * own_ref[...]
    for side, ref in enumerate((near_ref, far_ref)):
        columns = []
        for j in range(across):
            column = jnp.concatenate(
                [
                    summed_ref[step * m + TILE * side : step * m + TILE * (side + 1), :]
                    for m in range(j, group // TILE * across, across)
                ]
            )
            scale = scales_of(side * across + j)
            columns.append((0.5 / total_rows) * (column * mine * scale) * scale)
        mixing = jnp.concatenate(columns, axis=1)
        result = result - product(split(mixing), split(ref[...]), ((1,), (0,)))
    out_ref[...] = result


def call(kernel, out_shape, scalars, *arrays):
    vmem = pl.BlockSpec(memory_space=pltpu.VMEM)
    smem = pl.BlockSpec(memory_space=pltpu.SMEM)
    return pl.pallas_call(
        kernel,
        out_shape=jax.ShapeDtypeStruct(out_shape, jnp.float32),
        in_specs=[smem] * len(scalars) + [vmem] * len(arrays),
        out_specs=vmem,
        compiler_params=pltpu.CompilerParams(vmem_limit_bytes=24 * 2**20),
        interpret=INTERPRET,
    )(*scalars, *arrays)


def local(diag_blocks, coupling, vectors):
    count, width = vectors.shape
    blocks, size = diag_blocks.shape[0], diag_blocks.shape[1]
    nyl, nx, _ = (lax.axis_size(a) for a in VEC)
    total_rows = width * lax.axis_size(ROW)
    at, vectors = lax.optimization_barrier((lax.axis_index("x").reshape(1), vectors))
    flip = flipped(lax.axis_index("yh"), lax.axis_index("z"))
    yl = lax.axis_index("yl")
    chunk = jnp.where(flip, nyl - 1 - yl, yl)
    part, group, depth = blocks // nyl, nyl * count, width // nyl
    chunks = vectors.reshape(count, nyl, depth).transpose(1, 0, 2)
    chunks = jnp.where(flip, chunks[::-1], chunks)
    own = lax.all_to_all(chunks, "yl", split_axis=0, concat_axis=0, tiled=True)
    own = own.reshape(group, depth)
    own = jnp.concatenate(
        chebyshev(
            [own[:, n * size : (n + 1) * size] for n in range(part)],
            lax.dynamic_slice_in_dim(diag_blocks, chunk * part, part),
            lax.dynamic_slice_in_dim(coupling, chunk * part, part),
            chunk % 2 == 1,
        ),
        axis=1,
    )
    copies = jnp.broadcast_to(own[None], (nx, group, depth))
    near = lax.all_to_all(copies, "x", split_axis=0, concat_axis=0, tiled=True)
    near = near.reshape(nx * group, depth)
    far = lax.ppermute(near, "c", [(0, 1), (1, 0)])
    members = group // TILE * nx
    packed = (members * (2 * TILE + 1), LANES)

    def exchange(a):
        a = a.reshape(lax.axis_size(SUM), -1)
        return lax.all_to_all(a, SUM, split_axis=0, concat_axis=0, tiled=True).reshape(packed)

    pieces = exchange(call(gram_kernel, packed, (), own, near, far))
    summed = exchange(call(sum_kernel, packed, (), pieces))
    renewed = call(
        functools.partial(mixing_kernel, total_rows), (group, depth), (at,), summed, own, near, far
    )
    back = renewed.reshape(nyl, count, depth)
    back = lax.all_to_all(back, "yl", split_axis=0, concat_axis=0, tiled=True)
    back = jnp.where(flip, back[::-1], back)
    return back.transpose(1, 0, 2).reshape(count, width)


def solution(mesh):
    sizes = tuple(size for _, size in SPLIT)
    fine = Mesh(mesh.devices.reshape(sizes), tuple(name for name, _ in SPLIT))
    placed = (P(ROW, None, None), P(ROW, None, None), P(VEC, ROW))
    return jax.shard_map(
        local, mesh=fine, in_specs=placed, out_specs=P(VEC, ROW), check_vma=False
    )
```

```python
import functools

import jax
import jax.numpy as jnp
from jax import lax
from jax.experimental import pallas as pl
from jax.experimental.pallas import tpu as pltpu
from jax.sharding import Mesh, PartitionSpec as P


DEGREE = 4

filter_center = 0.1
filter_half = 1.0
epsilon = 1e-06
precision = lax.Precision.HIGH

SPLIT = (("yl", 4), ("x", 4), ("c", 2), ("yh", 2), ("z", 8))
VEC = ("yl", "x", "c")
ROW = ("yh", "z")
SUM = ("yl", "yh", "z")

TILE, LANES = 8, 128
INTERPRET = False


def dot(a, b, contract, batch=((), ())):
    return lax.dot_general(a, b, (contract, batch), precision=precision)


def flipped(yh, z):
    return (yh + z) % 2 == 0


def snake():
    nyl, nyh, nz = (lax.axis_size(a) for a in SUM)
    places = []
    for yh in range(nyh):
        for z in range(nz):
            order = range(nyl)
            for yl in reversed(order) if flipped(yh, z) else order:
                places.append((yl * nyh + yh) * nz + z)
    return places


def local_terms(y, diag_blocks, coupling):
    terms = []
    for n, block in enumerate(y):
        term = dot(block, diag_blocks[n], ((1,), (1,))) - filter_center * block
        if n + 1 < len(y):
            term = term + dot(y[n + 1], coupling[n], ((1,), (1,)))
        if n > 0:
            term = term + dot(y[n - 1], coupling[n - 1], ((1,), (0,)))
        terms.append(term)
    return terms


def edge_coupling(coupling, chunk):
    places = snake()
    nyl = lax.axis_size("yl")
    crossings = [(places[i - 1], places[i]) for i in range(nyl, len(places), nyl)]
    crossed = lax.ppermute(coupling[-1], SUM, crossings)
    part = coupling.shape[0] // nyl
    inside = lax.dynamic_index_in_dim(
        coupling, jnp.maximum(chunk * part - 1, 0), axis=0, keepdims=False
    )
    return jnp.where(chunk == 0, crossed, inside)


def chebyshev(y, diag_blocks, coupling, below, is_odd, is_top):
    places = snake()
    swaps = []
    for start in (1, 0):
        ups = [(places[i], places[i + 1]) for i in range(start, len(places) - 1, 2)]
        swaps.append(ups + [(above, below) for below, above in ups])
    top = coupling[-1]
    previous = None
    for turn in range(0, DEGREE, 2):
        scale = (1.0 if turn == 0 else 2.0) / filter_half
        a = [scale * term for term in local_terms(y, diag_blocks, coupling)]
        if previous is not None:
            a = [term - old for term, old in zip(a, previous)]
        term_up = dot(y[-1], top, ((1,), (0,)))
        up = jnp.concatenate([term_up, dot(a[-1], top, ((1,), (0,)))])
        down = jnp.concatenate([y[0], a[0]])
        odd = lax.ppermute(jnp.where(is_odd, up, down), SUM, swaps[0])
        even = lax.ppermute(jnp.where(is_odd, down, up), SUM, swaps[1])
        around = scale * dot(dot(y[0], below, ((1,), (1,))), below, ((1,), (0,)))
        above_y, above_a = jnp.split(jnp.where(is_odd, odd, even), 2)
        below_y, below_a = jnp.split(jnp.where(is_odd, even, odd), 2)
        a[-1] = a[-1] + scale * dot(above_y, top, ((1,), (1,)))
        a[0] = a[0] + scale * below_y
        above_a = jnp.where(is_top, 0.0, above_a + scale * term_up)
        below_a = below_a + around
        b = [(2.0 / filter_half) * term - old for term, old in zip(local_terms(a, diag_blocks, coupling), y)]
        b[-1] = b[-1] + (2.0 / filter_half) * dot(above_a, top, ((1,), (1,)))
        b[0] = b[0] + (2.0 / filter_half) * below_a
        previous, y = a, b
    return y


def split(a):
    high = a.astype(jnp.bfloat16)
    return high, (a - high.astype(jnp.float32)).astype(jnp.bfloat16)


def product(a, b, contract):
    def one(x, y):
        return lax.dot_general(x, y, (contract, ((), ())), preferred_element_type=jnp.float32)

    return one(a[0], b[0]) + (one(a[0], b[1]) + one(a[1], b[0]))


def gram_kernel(own_ref, near_ref, far_ref, out_ref):
    own = split(own_ref[...])
    ones = jnp.ones((TILE, own_ref.shape[1]), jnp.bfloat16)
    tiles, squares = [], []
    for ref in (near_ref, far_ref):
        tiles.append(product(own, split(ref[...]), ((1,), (1,))))
        square = split(ref[...] * ref[...])
        sums = [
            lax.dot_general(ones, part, (((1,), (1,)), ((), ())), preferred_element_type=jnp.float32)
            for part in square
        ]
        squares.append(sums[0] + sums[1])
    across = near_ref.shape[0] // LANES
    step = 2 * TILE + 1
    for m in range(out_ref.shape[0] // step):
        i, j = m // across * TILE, m % across * LANES
        for side in range(2):
            out_ref[step * m + TILE * side : step * m + TILE * (side + 1), :] = tiles[side][
                i : i + TILE, j : j + LANES
            ]
        side, j = m % (2 * across) // across, m % across * LANES
        out_ref[step * m + 2 * TILE : step * (m + 1), :] = squares[side][:1, j : j + LANES]


def sum_kernel(in_ref, out_ref):
    step = 2 * TILE + 1
    group = TILE * step
    count = in_ref.shape[0] // group
    total = in_ref[:group, :]
    for g in range(1, count):
        total = total + in_ref[group * g : group * (g + 1), :]
    out_ref[:group, :] = total
    piece = out_ref[:step, :]
    for m in range(1, TILE):
        piece = piece + out_ref[step * m : step * (m + 1), :]
    for m in range(TILE):
        out_ref[step * m : step * (m + 1), :] = piece
    total = out_ref[:group, :]
    for g in range(1, count):
        out_ref[group * g : group * (g + 1), :] = total


def mixing_kernel(total_rows, at_ref, summed_ref, own_ref, near_ref, far_ref, out_ref):
    step = 2 * TILE + 1
    across = near_ref.shape[0] // LANES
    group = own_ref.shape[0]

    def scales_of(m):
        row = summed_ref[pl.ds(step * m + 2 * TILE, 1), :]
        return 1.0 / jnp.sqrt(row / total_rows + epsilon)

    on_diagonal = lax.broadcasted_iota(jnp.int32, (group, LANES), 0) == (
        lax.broadcasted_iota(jnp.int32, (group, LANES), 1)
    )
    mine = jnp.sum(jnp.where(on_diagonal, scales_of(at_ref[0]), 0.0), axis=1, keepdims=True)
    result = 1.5 * mine * own_ref[...]
    for side, ref in enumerate((near_ref, far_ref)):
        columns = []
        for j in range(across):
            column = jnp.concatenate(
                [
                    summed_ref[step * m + TILE * side : step * m + TILE * (side + 1), :]
                    for m in range(j, group // TILE * across, across)
                ]
            )
            scale = scales_of(side * across + j)
            columns.append((0.5 / total_rows) * (column * mine * scale) * scale)
        mixing = jnp.concatenate(columns, axis=1)
        result = result - product(split(mixing), split(ref[...]), ((1,), (0,)))
    out_ref[...] = result


def call(kernel, out_shape, scalars, *arrays):
    vmem = pl.BlockSpec(memory_space=pltpu.VMEM)
    smem = pl.BlockSpec(memory_space=pltpu.SMEM)
    return pl.pallas_call(
        kernel,
        out_shape=jax.ShapeDtypeStruct(out_shape, jnp.float32),
        in_specs=[smem] * len(scalars) + [vmem] * len(arrays),
        out_specs=vmem,
        compiler_params=pltpu.CompilerParams(vmem_limit_bytes=24 * 2**20),
        interpret=INTERPRET,
    )(*scalars, *arrays)


def local(diag_blocks, coupling, vectors):
    count, width = vectors.shape
    blocks, size = diag_blocks.shape[0], diag_blocks.shape[1]
    nyl, nx, _ = (lax.axis_size(a) for a in VEC)
    total_rows = width * lax.axis_size(ROW)
    at, vectors = lax.optimization_barrier((lax.axis_index("x").reshape(1), vectors))
    flip = flipped(lax.axis_index("yh"), lax.axis_index("z"))
    yl = lax.axis_index("yl")
    chunk = jnp.where(flip, nyl - 1 - yl, yl)
    part, group, depth = blocks // nyl, nyl * count, width // nyl
    chunks = vectors.reshape(count, nyl, depth).transpose(1, 0, 2)
    chunks = jnp.where(flip, chunks[::-1], chunks)
    own = lax.all_to_all(chunks, "yl", split_axis=0, concat_axis=0, tiled=True)
    own = own.reshape(group, depth)
    own = jnp.concatenate(
        chebyshev(
            [own[:, n * size : (n + 1) * size] for n in range(part)],
            lax.dynamic_slice_in_dim(diag_blocks, chunk * part, part),
            lax.dynamic_slice_in_dim(coupling, chunk * part, part),
            edge_coupling(coupling, chunk),
            chunk % 2 == 1,
            (lax.axis_index(ROW) == lax.axis_size(ROW) - 1) & (chunk == nyl - 1),
        ),
        axis=1,
    )
    copies = jnp.broadcast_to(own[None], (nx, group, depth))
    near = lax.all_to_all(copies, "x", split_axis=0, concat_axis=0, tiled=True)
    near = near.reshape(nx * group, depth)
    far = lax.ppermute(near, "c", [(0, 1), (1, 0)])
    members = group // TILE * nx
    packed = (members * (2 * TILE + 1), LANES)

    def exchange(a):
        a = a.reshape(lax.axis_size(SUM), -1)
        return lax.all_to_all(a, SUM, split_axis=0, concat_axis=0, tiled=True).reshape(packed)

    pieces = exchange(call(gram_kernel, packed, (), own, near, far))
    summed = exchange(call(sum_kernel, packed, (), pieces))
    renewed = call(
        functools.partial(mixing_kernel, total_rows), (group, depth), (at,), summed, own, near, far
    )
    back = renewed.reshape(nyl, count, depth)
    back = lax.all_to_all(back, "yl", split_axis=0, concat_axis=0, tiled=True)
    back = jnp.where(flip, back[::-1], back)
    return back.transpose(1, 0, 2).reshape(count, width)


def solution(mesh):
    sizes = tuple(size for _, size in SPLIT)
    fine = Mesh(mesh.devices.reshape(sizes), tuple(name for name, _ in SPLIT))
    placed = (P(ROW, None, None), P(ROW, None, None), P(VEC, ROW))
    return jax.shard_map(
        local, mesh=fine, in_specs=placed, out_specs=P(VEC, ROW), check_vma=False
    )
```

```python
import functools

import jax
import jax.numpy as jnp
from jax import lax
from jax.experimental import pallas as pl
from jax.experimental.pallas import tpu as pltpu
from jax.sharding import Mesh, PartitionSpec as P


DEGREE = 4

filter_center = 0.1
filter_half = 1.0
epsilon = 1e-06
precision = lax.Precision.HIGH

SPLIT = (("yl", 4), ("x", 4), ("c", 2), ("yh", 2), ("z", 8))
VEC = ("yl", "x", "c")
ROW = ("yh", "z")
SUM = ("yl", "yh", "z")

TILE, LANES = 8, 128
INTERPRET = False


def dot(a, b, contract, batch=((), ())):
    return lax.dot_general(a, b, (contract, batch), precision=precision)


def flipped(yh, z):
    return (yh + z) % 2 == 0


def snake():
    nyl, nyh, nz = (lax.axis_size(a) for a in SUM)
    places = []
    for yh in range(nyh):
        for z in range(nz):
            order = range(nyl)
            for yl in reversed(order) if flipped(yh, z) else order:
                places.append((yl * nyh + yh) * nz + z)
    return places


def edge_coupling(coupling, chunk):
    places = snake()
    nyl = lax.axis_size("yl")
    crossings = [(places[i - 1], places[i]) for i in range(nyl, len(places), nyl)]
    crossed = lax.ppermute(coupling[-1], SUM, crossings)
    part = coupling.shape[0] // nyl
    inside = lax.dynamic_index_in_dim(
        coupling, jnp.maximum(chunk * part - 1, 0), axis=0, keepdims=False
    )
    return jnp.where(chunk == 0, crossed, inside)


def split(a):
    high = a.astype(jnp.bfloat16)
    return high, (a - high.astype(jnp.float32)).astype(jnp.bfloat16)


def product(a, b, contract):
    def one(x, y):
        return lax.dot_general(x, y, (contract, ((), ())), preferred_element_type=jnp.float32)

    return one(a[0], b[0]) + (one(a[0], b[1]) + one(a[1], b[0]))


def blocks_of(ref, size):
    return [ref[:, n : n + size] for n in range(0, ref.shape[1], size)]


def local_terms(y, parts, diagonal, coupling):
    terms = []
    for n, block in enumerate(y):
        term = product(parts[n], diagonal(n), ((1,), (1,))) - filter_center * block
        if n + 1 < len(y):
            term = term + product(parts[n + 1], coupling(n), ((1,), (1,)))
        if n > 0:
            term = term + product(parts[n - 1], coupling(n - 1), ((1,), (0,)))
        terms.append(term)
    return terms


def send(is_odd, y, parts, a, top, odd_ref, even_ref, term_ref):
    rows = y[0].shape[0]
    term_up = product(parts[-1], top, ((1,), (0,)))
    term_ref[...] = term_up
    up = (term_up, product(split(a[-1]), top, ((1,), (0,))))
    down = (y[0], a[0])
    for holds, up_ref, down_ref in (
        (is_odd, odd_ref, even_ref),
        (jnp.logical_not(is_odd), even_ref, odd_ref),
    ):

        @pl.when(holds)
        def _(up_ref=up_ref, down_ref=down_ref):
            for ref, pair in ((up_ref, up), (down_ref, down)):
                ref[:rows, :] = pair[0]
                ref[rows:, :] = pair[1]


def start_kernel(flags, y_ref, d_ref, c_ref, dh, dl, ch, cl, a_ref, odd_ref, even_ref, term_ref):
    for ref, high, low in ((d_ref, dh, dl), (c_ref, ch, cl)):
        for n in range(ref.shape[0]):
            high[n], low[n] = split(ref[n])
    size = d_ref.shape[1]
    y = blocks_of(y_ref, size)
    parts = [split(block) for block in y]
    coupling = lambda n: (ch[n], cl[n])
    a = local_terms(y, parts, lambda n: (dh[n], dl[n]), coupling)
    a = [term / filter_half for term in a]
    a_ref[...] = jnp.concatenate(a, axis=1)
    send(flags[0] == 1, y, parts, a, coupling(len(y) - 1), odd_ref, even_ref, term_ref)


def step_kernel(
    scale,
    flags,
    y_ref,
    a_ref,
    got_odd,
    got_even,
    around_ref,
    got_term,
    dh,
    dl,
    ch,
    cl,
    b_ref,
    next_ref=None,
    odd_ref=None,
    even_ref=None,
    term_ref=None,
):
    size = dh.shape[1]
    double = 2.0 / filter_half
    is_odd = flags[0] == 1
    diagonal, coupling = lambda n: (dh[n], dl[n]), lambda n: (ch[n], cl[n])
    y, a = blocks_of(y_ref, size), blocks_of(a_ref, size)
    top = coupling(len(y) - 1)
    rows = y[0].shape[0]

    def above(rows_of):
        return jnp.where(is_odd, got_odd[rows_of, :], got_even[rows_of, :])

    def below(rows_of):
        return jnp.where(is_odd, got_even[rows_of, :], got_odd[rows_of, :])

    edge, part = slice(0, rows), slice(rows, 2 * rows)
    a[-1] = a[-1] + scale * product(split(above(edge)), top, ((1,), (1,)))
    a[0] = a[0] + scale * below(edge)
    above_a = jnp.where(flags[1] == 1, 0.0, above(part) + scale * got_term[...])
    below_a = below(part) + around_ref[...]
    terms = local_terms(a, [split(block) for block in a], diagonal, coupling)
    b = [double * term - old for term, old in zip(terms, y)]
    b[-1] = b[-1] + double * product(split(above_a), top, ((1,), (1,)))
    b[0] = b[0] + double * below_a
    b_ref[...] = jnp.concatenate(b, axis=1)
    if next_ref is not None:
        parts = [split(block) for block in b]
        terms = local_terms(b, parts, diagonal, coupling)
        a = [double * term - old for term, old in zip(terms, a)]
        next_ref[...] = jnp.concatenate(a, axis=1)
        send(is_odd, b, parts, a, top, odd_ref, even_ref, term_ref)


def chebyshev(y, diag_blocks, coupling, below, flags):
    places = snake()
    swaps = []
    for start in (1, 0):
        ups = [(places[i], places[i + 1]) for i in range(start, len(places) - 1, 2)]
        swaps.append(ups + [(above, below) for below, above in ups])
    rows, size = y.shape[0], diag_blocks.shape[1]
    message = jax.ShapeDtypeStruct((2 * rows, size), jnp.float32)
    panel = jax.ShapeDtypeStruct(y.shape, jnp.float32)
    sends = [panel, message, message, jax.ShapeDtypeStruct((rows, size), jnp.float32)]
    halves = [jax.ShapeDtypeStruct(diag_blocks.shape, jnp.bfloat16)] * 4
    *hamiltonian, a, odd, even, term = call(
        start_kernel, halves + sends, (flags,), y, diag_blocks, coupling
    )
    for turn in range(0, DEGREE, 2):
        scale = (1.0 if turn == 0 else 2.0) / filter_half
        odd = lax.ppermute(odd, SUM, swaps[0])
        even = lax.ppermute(even, SUM, swaps[1])
        around = scale * dot(
            dot(y[:, :size], below, ((1,), (1,))), below, ((1,), (0,))
        )
        final = turn + 2 >= DEGREE
        result = call(
            functools.partial(step_kernel, scale),
            [panel] if final else [panel] + sends,
            (flags,),
            y,
            a,
            odd,
            even,
            around,
            term,
            *hamiltonian,
        )
        y = result[0]
        if not final:
            a, odd, even, term = result[1:]
    return y


def spread_kernel(flip, in_ref, out_ref, sems):
    count, _, depth = out_ref.shape
    copies = []
    for j in range(count):
        at = jnp.where(flip[0] == 1, count - 1 - j, j) * depth
        source = in_ref.at[:, pl.ds(pl.multiple_of(at, depth), depth)]
        copies.append(pltpu.make_async_copy(source, out_ref.at[j], sems.at[j]))
    for copy in copies:
        copy.start()
    for copy in copies:
        copy.wait()


def spread(flip, vectors, count):
    rows, width = vectors.shape
    return pl.pallas_call(
        spread_kernel,
        out_shape=jax.ShapeDtypeStruct((count, rows, width // count), jnp.float32),
        in_specs=[
            pl.BlockSpec(memory_space=pltpu.SMEM),
            pl.BlockSpec(memory_space=pl.ANY),
        ],
        out_specs=pl.BlockSpec(memory_space=pltpu.VMEM),
        scratch_shapes=[pltpu.SemaphoreType.DMA((count,))],
        name="spread",
        compiler_params=pltpu.CompilerParams(vmem_limit_bytes=24 * 2**20),
        interpret=INTERPRET,
    )(flip, vectors)


def gram_kernel(own_ref, near_ref, far_ref, out_ref):
    own = split(own_ref[...])
    ones = jnp.ones((TILE, own_ref.shape[1]), jnp.bfloat16)
    tiles, squares = [], []
    for ref in (near_ref, far_ref):
        tiles.append(product(own, split(ref[...]), ((1,), (1,))))
        square = split(ref[...] * ref[...])
        sums = [
            lax.dot_general(ones, part, (((1,), (1,)), ((), ())), preferred_element_type=jnp.float32)
            for part in square
        ]
        squares.append(sums[0] + sums[1])
    across = near_ref.shape[0] // LANES
    step = 2 * TILE + 1
    for m in range(out_ref.shape[0] // step):
        i, j = m // across * TILE, m % across * LANES
        for side in range(2):
            out_ref[step * m + TILE * side : step * m + TILE * (side + 1), :] = tiles[side][
                i : i + TILE, j : j + LANES
            ]
        side, j = m % (2 * across) // across, m % across * LANES
        out_ref[step * m + 2 * TILE : step * (m + 1), :] = squares[side][:1, j : j + LANES]


def sum_kernel(in_ref, out_ref):
    step = 2 * TILE + 1
    group = TILE * step
    count = in_ref.shape[0] // group
    total = in_ref[:group, :]
    for g in range(1, count):
        total = total + in_ref[group * g : group * (g + 1), :]
    out_ref[:group, :] = total
    piece = out_ref[:step, :]
    for m in range(1, TILE):
        piece = piece + out_ref[step * m : step * (m + 1), :]
    for m in range(TILE):
        out_ref[step * m : step * (m + 1), :] = piece
    total = out_ref[:group, :]
    for g in range(1, count):
        out_ref[group * g : group * (g + 1), :] = total


def mixing_kernel(total_rows, at_ref, summed_ref, own_ref, near_ref, far_ref, out_ref):
    step = 2 * TILE + 1
    across = near_ref.shape[0] // LANES
    group = own_ref.shape[0]

    def scales_of(m):
        row = summed_ref[pl.ds(step * m + 2 * TILE, 1), :]
        return 1.0 / jnp.sqrt(row / total_rows + epsilon)

    on_diagonal = lax.broadcasted_iota(jnp.int32, (group, LANES), 0) == (
        lax.broadcasted_iota(jnp.int32, (group, LANES), 1)
    )
    mine = jnp.sum(jnp.where(on_diagonal, scales_of(at_ref[0]), 0.0), axis=1, keepdims=True)
    result = 1.5 * mine * own_ref[...]
    for side, ref in enumerate((near_ref, far_ref)):
        columns = []
        for j in range(across):
            column = jnp.concatenate(
                [
                    summed_ref[step * m + TILE * side : step * m + TILE * (side + 1), :]
                    for m in range(j, group // TILE * across, across)
                ]
            )
            scale = scales_of(side * across + j)
            columns.append((0.5 / total_rows) * (column * mine * scale) * scale)
        mixing = jnp.concatenate(columns, axis=1)
        result = result - product(split(mixing), split(ref[...]), ((1,), (0,)))
    out_ref[...] = result


def call(kernel, out_shapes, scalars, *arrays):
    vmem = pl.BlockSpec(memory_space=pltpu.VMEM)
    smem = pl.BlockSpec(memory_space=pltpu.SMEM)
    return pl.pallas_call(
        kernel,
        out_shape=out_shapes,
        in_specs=[smem] * len(scalars) + [vmem] * len(arrays),
        out_specs=[vmem] * len(out_shapes),
        compiler_params=pltpu.CompilerParams(vmem_limit_bytes=24 * 2**20),
        interpret=INTERPRET,
    )(*scalars, *arrays)


def local(diag_blocks, coupling, vectors):
    count, width = vectors.shape
    blocks = diag_blocks.shape[0]
    nyl, nx, _ = (lax.axis_size(a) for a in VEC)
    total_rows = width * lax.axis_size(ROW)
    at, vectors = lax.optimization_barrier((lax.axis_index("x").reshape(1), vectors))
    flip = flipped(lax.axis_index("yh"), lax.axis_index("z"))
    yl = lax.axis_index("yl")
    chunk = jnp.where(flip, nyl - 1 - yl, yl)
    part, group, depth = blocks // nyl, nyl * count, width // nyl
    chunks = spread(flip.astype(jnp.int32).reshape(1), vectors, nyl)
    own = lax.all_to_all(chunks, "yl", split_axis=0, concat_axis=0, tiled=True)
    own = own.reshape(group, depth)
    is_top = (lax.axis_index(ROW) == lax.axis_size(ROW) - 1) & (chunk == nyl - 1)
    own_diag = lax.dynamic_slice_in_dim(diag_blocks, chunk * part, part)
    own_coupling = lax.dynamic_slice_in_dim(coupling, chunk * part, part)
    own = chebyshev(
        own,
        own_diag,
        own_coupling,
        edge_coupling(coupling, chunk),
        jnp.stack([chunk % 2, is_top.astype(jnp.int32)]),
    )
    copies = jnp.broadcast_to(own[None], (nx, group, depth))
    near = lax.all_to_all(copies, "x", split_axis=0, concat_axis=0, tiled=True)
    near = near.reshape(nx * group, depth)
    far = lax.ppermute(near, "c", [(0, 1), (1, 0)])
    members = group // TILE * nx
    packed = (members * (2 * TILE + 1), LANES)
    packed_type = jax.ShapeDtypeStruct(packed, jnp.float32)

    def exchange(a):
        a = a.reshape(lax.axis_size(SUM), -1)
        return lax.all_to_all(a, SUM, split_axis=0, concat_axis=0, tiled=True).reshape(packed)

    pieces = exchange(call(gram_kernel, [packed_type], (), own, near, far)[0])
    summed = exchange(call(sum_kernel, [packed_type], (), pieces)[0])
    renewed = call(
        functools.partial(mixing_kernel, total_rows),
        [jax.ShapeDtypeStruct((group, depth), jnp.float32)],
        (at,),
        summed,
        own,
        near,
        far,
    )[0]
    back = renewed.reshape(nyl, count, depth)
    back = lax.all_to_all(back, "yl", split_axis=0, concat_axis=0, tiled=True)
    back = jnp.where(flip, back[::-1], back)
    return back.transpose(1, 0, 2).reshape(count, width)


def solution(mesh):
    sizes = tuple(size for _, size in SPLIT)
    fine = Mesh(mesh.devices.reshape(sizes), tuple(name for name, _ in SPLIT))
    placed = (P(ROW, None, None), P(ROW, None, None), P(VEC, ROW))
    return jax.shard_map(
        local, mesh=fine, in_specs=placed, out_specs=P(VEC, ROW), check_vma=False
    )
```

```python
import functools

import jax
import jax.numpy as jnp
from jax import lax
from jax.experimental import pallas as pl
from jax.experimental.pallas import tpu as pltpu
from jax.sharding import Mesh, PartitionSpec as P


DEGREE = 4

filter_center = 0.1
filter_half = 1.0
epsilon = 1e-06
precision = lax.Precision.HIGH

SPLIT = (("yl", 4), ("x", 4), ("c", 2), ("yh", 2), ("z", 8))
VEC = ("yl", "x", "c")
ROW = ("yh", "z")
SUM = ("yl", "yh", "z")

TILE, LANES = 8, 128
INTERPRET = False


def dot(a, b, contract, batch=((), ())):
    return lax.dot_general(a, b, (contract, batch), precision=precision)


def flipped(yh, z):
    return (yh + z) % 2 == 0


def snake():
    nyl, nyh, nz = (lax.axis_size(a) for a in SUM)
    places = []
    for yh in range(nyh):
        for z in range(nz):
            order = range(nyl)
            for yl in reversed(order) if flipped(yh, z) else order:
                places.append((yl * nyh + yh) * nz + z)
    return places


def edge_coupling(coupling, chunk):
    places = snake()
    nyl = lax.axis_size("yl")
    crossings = [(places[i - 1], places[i]) for i in range(nyl, len(places), nyl)]
    crossed = lax.ppermute(coupling[-1], SUM, crossings)
    part = coupling.shape[0] // nyl
    inside = lax.dynamic_index_in_dim(
        coupling, jnp.maximum(chunk * part - 1, 0), axis=0, keepdims=False
    )
    return jnp.where(chunk == 0, crossed, inside)


def split(a):
    high = a.astype(jnp.bfloat16)
    return high, (a - high.astype(jnp.float32)).astype(jnp.bfloat16)


def product(a, b, contract):
    def one(x, y):
        return lax.dot_general(x, y, (contract, ((), ())), preferred_element_type=jnp.float32)

    return one(a[0], b[0]) + (one(a[0], b[1]) + one(a[1], b[0]))


def blocks_of(ref, size):
    return [ref[:, n : n + size] for n in range(0, ref.shape[1], size)]


def local_terms(y, parts, diagonal, coupling):
    terms = []
    for n, block in enumerate(y):
        term = product(parts[n], diagonal(n), ((1,), (1,))) - filter_center * block
        if n + 1 < len(y):
            term = term + product(parts[n + 1], coupling(n), ((1,), (1,)))
        if n > 0:
            term = term + product(parts[n - 1], coupling(n - 1), ((1,), (0,)))
        terms.append(term)
    return terms


def send(is_odd, y, parts, a, top, odd_ref, even_ref, term_ref):
    rows = y[0].shape[0]
    term_up = product(parts[-1], top, ((1,), (0,)))
    term_ref[...] = term_up
    up = (term_up, product(split(a[-1]), top, ((1,), (0,))))
    down = (y[0], a[0])
    for holds, up_ref, down_ref in (
        (is_odd, odd_ref, even_ref),
        (jnp.logical_not(is_odd), even_ref, odd_ref),
    ):

        @pl.when(holds)
        def _(up_ref=up_ref, down_ref=down_ref):
            for ref, pair in ((up_ref, up), (down_ref, down)):
                ref[:rows, :] = pair[0]
                ref[rows:, :] = pair[1]


def start_kernel(flags, y_ref, d_ref, c_ref, dh, dl, ch, cl, a_ref, odd_ref, even_ref, term_ref):
    for ref, high, low in ((d_ref, dh, dl), (c_ref, ch, cl)):
        for n in range(ref.shape[0]):
            high[n], low[n] = split(ref[n])
    size = d_ref.shape[1]
    y = blocks_of(y_ref, size)
    parts = [split(block) for block in y]
    coupling = lambda n: (ch[n], cl[n])
    a = local_terms(y, parts, lambda n: (dh[n], dl[n]), coupling)
    a = [term / filter_half for term in a]
    a_ref[...] = jnp.concatenate(a, axis=1)
    send(flags[0] == 1, y, parts, a, coupling(len(y) - 1), odd_ref, even_ref, term_ref)


def step_kernel(
    scale,
    flags,
    y_ref,
    a_ref,
    got_odd,
    got_even,
    around_ref,
    got_term,
    dh,
    dl,
    ch,
    cl,
    b_ref,
    next_ref=None,
    odd_ref=None,
    even_ref=None,
    term_ref=None,
):
    size = dh.shape[1]
    double = 2.0 / filter_half
    is_odd = flags[0] == 1
    diagonal, coupling = lambda n: (dh[n], dl[n]), lambda n: (ch[n], cl[n])
    y, a = blocks_of(y_ref, size), blocks_of(a_ref, size)
    top = coupling(len(y) - 1)
    rows = y[0].shape[0]

    def above(rows_of):
        return jnp.where(is_odd, got_odd[rows_of, :], got_even[rows_of, :])

    def below(rows_of):
        return jnp.where(is_odd, got_even[rows_of, :], got_odd[rows_of, :])

    edge, part = slice(0, rows), slice(rows, 2 * rows)
    a[-1] = a[-1] + scale * product(split(above(edge)), top, ((1,), (1,)))
    a[0] = a[0] + scale * below(edge)
    above_a = jnp.where(flags[1] == 1, 0.0, above(part) + scale * got_term[...])
    below_a = below(part) + around_ref[...]
    terms = local_terms(a, [split(block) for block in a], diagonal, coupling)
    b = [double * term - old for term, old in zip(terms, y)]
    b[-1] = b[-1] + double * product(split(above_a), top, ((1,), (1,)))
    b[0] = b[0] + double * below_a
    b_ref[...] = jnp.concatenate(b, axis=1)
    if next_ref is not None:
        parts = [split(block) for block in b]
        terms = local_terms(b, parts, diagonal, coupling)
        a = [double * term - old for term, old in zip(terms, a)]
        next_ref[...] = jnp.concatenate(a, axis=1)
        send(is_odd, b, parts, a, top, odd_ref, even_ref, term_ref)


def chebyshev(y, diag_blocks, coupling, below, flags):
    places = snake()
    swaps = []
    for start in (1, 0):
        ups = [(places[i], places[i + 1]) for i in range(start, len(places) - 1, 2)]
        swaps.append(ups + [(above, below) for below, above in ups])
    rows, size = y.shape[0], diag_blocks.shape[1]
    message = jax.ShapeDtypeStruct((2 * rows, size), jnp.float32)
    panel = jax.ShapeDtypeStruct(y.shape, jnp.float32)
    sends = [panel, message, message, jax.ShapeDtypeStruct((rows, size), jnp.float32)]
    halves = [jax.ShapeDtypeStruct(diag_blocks.shape, jnp.bfloat16)] * 4
    *hamiltonian, a, odd, even, term = call(
        start_kernel, halves + sends, (flags,), y, diag_blocks, coupling
    )
    for turn in range(0, DEGREE, 2):
        scale = (1.0 if turn == 0 else 2.0) / filter_half
        odd = lax.ppermute(odd, SUM, swaps[0])
        even = lax.ppermute(even, SUM, swaps[1])
        around = scale * dot(
            dot(y[:, :size], below, ((1,), (1,))), below, ((1,), (0,))
        )
        final = turn + 2 >= DEGREE
        result = call(
            functools.partial(step_kernel, scale),
            [panel] if final else [panel] + sends,
            (flags,),
            y,
            a,
            odd,
            even,
            around,
            term,
            *hamiltonian,
        )
        y = result[0]
        if not final:
            a, odd, even, term = result[1:]
    return y


def spread_kernel(flip, in_ref, out_ref, sems):
    count, _, depth = out_ref.shape
    copies = []
    for j in range(count):
        at = jnp.where(flip[0] == 1, count - 1 - j, j) * depth
        source = in_ref.at[:, pl.ds(pl.multiple_of(at, depth), depth)]
        copies.append(pltpu.make_async_copy(source, out_ref.at[j], sems.at[j]))
    for copy in copies:
        copy.start()
    for copy in copies:
        copy.wait()


def spread(flip, vectors, count):
    rows, width = vectors.shape
    return pl.pallas_call(
        spread_kernel,
        out_shape=jax.ShapeDtypeStruct((count, rows, width // count), jnp.float32),
        in_specs=[
            pl.BlockSpec(memory_space=pltpu.SMEM),
            pl.BlockSpec(memory_space=pltpu.HBM),
        ],
        out_specs=pl.BlockSpec(memory_space=pltpu.VMEM),
        scratch_shapes=[pltpu.SemaphoreType.DMA((count,))],
        name="spread",
        compiler_params=pltpu.CompilerParams(vmem_limit_bytes=24 * 2**20),
        interpret=INTERPRET,
    )(flip, vectors)


def gram_half(own_ref, ref):
    tiles = product(split(own_ref[...]), split(ref[...]), ((1,), (1,)))
    ones = jnp.ones((TILE, own_ref.shape[1]), jnp.bfloat16)
    sums = [
        lax.dot_general(ones, part, (((1,), (1,)), ((), ())), preferred_element_type=jnp.float32)
        for part in split(ref[...] * ref[...])
    ]
    return tiles, sums[0] + sums[1]


def near_kernel(own_ref, near_ref, tiles_ref, squares_ref):
    tiles_ref[...], squares_ref[...] = gram_half(own_ref, near_ref)


def gram_kernel(own_ref, tiles_ref, squares_ref, far_ref, out_ref):
    tiles, squares = zip((tiles_ref[...], squares_ref[...]), gram_half(own_ref, far_ref))
    across = far_ref.shape[0] // LANES
    step = 2 * TILE + 1
    for m in range(out_ref.shape[0] // step):
        i, j = m // across * TILE, m % across * LANES
        for side in range(2):
            out_ref[step * m + TILE * side : step * m + TILE * (side + 1), :] = tiles[side][
                i : i + TILE, j : j + LANES
            ]
        side, j = m % (2 * across) // across, m % across * LANES
        out_ref[step * m + 2 * TILE : step * (m + 1), :] = squares[side][:1, j : j + LANES]


def sum_kernel(in_ref, out_ref):
    step = 2 * TILE + 1
    group = TILE * step
    count = in_ref.shape[0] // group
    total = in_ref[:group, :]
    for g in range(1, count):
        total = total + in_ref[group * g : group * (g + 1), :]
    out_ref[:group, :] = total
    piece = out_ref[:step, :]
    for m in range(1, TILE):
        piece = piece + out_ref[step * m : step * (m + 1), :]
    for m in range(TILE):
        out_ref[step * m : step * (m + 1), :] = piece
    total = out_ref[:group, :]
    for g in range(1, count):
        out_ref[group * g : group * (g + 1), :] = total


def mixing_kernel(total_rows, at_ref, summed_ref, own_ref, near_ref, far_ref, out_ref):
    step = 2 * TILE + 1
    across = near_ref.shape[0] // LANES
    group = own_ref.shape[0]

    def scales_of(m):
        row = summed_ref[pl.ds(step * m + 2 * TILE, 1), :]
        return 1.0 / jnp.sqrt(row / total_rows + epsilon)

    on_diagonal = lax.broadcasted_iota(jnp.int32, (group, LANES), 0) == (
        lax.broadcasted_iota(jnp.int32, (group, LANES), 1)
    )
    mine = jnp.sum(jnp.where(on_diagonal, scales_of(at_ref[0]), 0.0), axis=1, keepdims=True)
    result = 1.5 * mine * own_ref[...]
    for side, ref in enumerate((near_ref, far_ref)):
        columns = []
        for j in range(across):
            column = jnp.concatenate(
                [
                    summed_ref[step * m + TILE * side : step * m + TILE * (side + 1), :]
                    for m in range(j, group // TILE * across, across)
                ]
            )
            scale = scales_of(side * across + j)
            columns.append((0.5 / total_rows) * (column * mine * scale) * scale)
        mixing = jnp.concatenate(columns, axis=1)
        result = result - product(split(mixing), split(ref[...]), ((1,), (0,)))
    out_ref[...] = result


def call(kernel, out_shapes, scalars, *arrays):
    vmem = pl.BlockSpec(memory_space=pltpu.VMEM)
    smem = pl.BlockSpec(memory_space=pltpu.SMEM)
    return pl.pallas_call(
        kernel,
        out_shape=out_shapes,
        in_specs=[smem] * len(scalars) + [vmem] * len(arrays),
        out_specs=[vmem] * len(out_shapes),
        compiler_params=pltpu.CompilerParams(vmem_limit_bytes=24 * 2**20),
        interpret=INTERPRET,
    )(*scalars, *arrays)


def local(diag_blocks, coupling, vectors):
    count, width = vectors.shape
    blocks = diag_blocks.shape[0]
    nyl, nx, _ = (lax.axis_size(a) for a in VEC)
    total_rows = width * lax.axis_size(ROW)
    at, vectors = lax.optimization_barrier((lax.axis_index("x").reshape(1), vectors))
    flip = flipped(lax.axis_index("yh"), lax.axis_index("z"))
    yl = lax.axis_index("yl")
    chunk = jnp.where(flip, nyl - 1 - yl, yl)
    part, group, depth = blocks // nyl, nyl * count, width // nyl
    chunks = spread(flip.astype(jnp.int32).reshape(1), vectors, nyl)
    own = lax.all_to_all(chunks, "yl", split_axis=0, concat_axis=0, tiled=True)
    own = own.reshape(group, depth)
    is_top = (lax.axis_index(ROW) == lax.axis_size(ROW) - 1) & (chunk == nyl - 1)
    own_diag = lax.dynamic_slice_in_dim(diag_blocks, chunk * part, part)
    own_coupling = lax.dynamic_slice_in_dim(coupling, chunk * part, part)
    own = chebyshev(
        own,
        own_diag,
        own_coupling,
        edge_coupling(coupling, chunk),
        jnp.stack([chunk % 2, is_top.astype(jnp.int32)]),
    )
    copies = jnp.broadcast_to(own[None], (nx, group, depth))
    near = lax.all_to_all(copies, "x", split_axis=0, concat_axis=0, tiled=True)
    near = near.reshape(nx * group, depth)
    far = lax.ppermute(near, "c", [(0, 1), (1, 0)])
    half_types = [jax.ShapeDtypeStruct((n, nx * group), jnp.float32) for n in (group, TILE)]
    halves = call(near_kernel, half_types, (), own, near)
    members = group // TILE * nx
    packed = (members * (2 * TILE + 1), LANES)
    packed_type = jax.ShapeDtypeStruct(packed, jnp.float32)

    def exchange(a):
        a = a.reshape(lax.axis_size(SUM), -1)
        return lax.all_to_all(a, SUM, split_axis=0, concat_axis=0, tiled=True).reshape(packed)

    pieces = exchange(call(gram_kernel, [packed_type], (), own, *halves, far)[0])
    summed = exchange(call(sum_kernel, [packed_type], (), pieces)[0])
    renewed = call(
        functools.partial(mixing_kernel, total_rows),
        [jax.ShapeDtypeStruct((group, depth), jnp.float32)],
        (at,),
        summed,
        own,
        near,
        far,
    )[0]
    back = renewed.reshape(nyl, count, depth)
    back = lax.all_to_all(back, "yl", split_axis=0, concat_axis=0, tiled=True)
    back = jnp.where(flip, back[::-1], back)
    return back.transpose(1, 0, 2).reshape(count, width)


def solution(mesh):
    sizes = tuple(size for _, size in SPLIT)
    fine = Mesh(mesh.devices.reshape(sizes), tuple(name for name, _ in SPLIT))
    placed = (P(ROW, None, None), P(ROW, None, None), P(VEC, ROW))
    return jax.shard_map(
        local, mesh=fine, in_specs=placed, out_specs=P(VEC, ROW), check_vma=False
    )
```

```python
import functools

import jax
import jax.numpy as jnp
from jax import lax
from jax.experimental import pallas as pl
from jax.experimental.pallas import tpu as pltpu
from jax.sharding import Mesh, PartitionSpec as P


DEGREE = 4

filter_center = 0.1
filter_half = 1.0
epsilon = 1e-06
precision = lax.Precision.HIGH

SPLIT = (("yl", 4), ("x", 4), ("c", 2), ("yh", 2), ("z", 8))
VEC = ("yl", "x", "c")
ROW = ("yh", "z")
SUM = ("yl", "yh", "z")

TILE, LANES = 8, 128
INTERPRET = False


def dot(a, b, contract, batch=((), ())):
    return lax.dot_general(a, b, (contract, batch), precision=precision)


def flipped(yh, z):
    return (yh + z) % 2 == 0


def snake():
    nyl, nyh, nz = (lax.axis_size(a) for a in SUM)
    places = []
    for yh in range(nyh):
        for z in range(nz):
            order = range(nyl)
            for yl in reversed(order) if flipped(yh, z) else order:
                places.append((yl * nyh + yh) * nz + z)
    return places


def edge_coupling(coupling, chunk):
    places = snake()
    nyl = lax.axis_size("yl")
    crossings = [(places[i - 1], places[i]) for i in range(nyl, len(places), nyl)]
    crossed = lax.ppermute(coupling[-1], SUM, crossings)
    part = coupling.shape[0] // nyl
    inside = lax.dynamic_index_in_dim(
        coupling, jnp.maximum(chunk * part - 1, 0), axis=0, keepdims=False
    )
    return jnp.where(chunk == 0, crossed, inside)


def split(a):
    high = a.astype(jnp.bfloat16)
    return high, (a - high.astype(jnp.float32)).astype(jnp.bfloat16)


def product(a, b, contract):
    def one(x, y):
        return lax.dot_general(x, y, (contract, ((), ())), preferred_element_type=jnp.float32)

    return one(a[0], b[0]) + (one(a[0], b[1]) + one(a[1], b[0]))


def blocks_of(ref, size):
    return [ref[:, n : n + size] for n in range(0, ref.shape[1], size)]


def local_terms(y, parts, diagonal, coupling):
    terms = []
    for n, block in enumerate(y):
        term = product(parts[n], diagonal(n), ((1,), (0,))) - filter_center * block
        if n + 1 < len(y):
            term = term + product(parts[n + 1], coupling(n), ((1,), (1,)))
        if n > 0:
            term = term + product(parts[n - 1], coupling(n - 1), ((1,), (0,)))
        terms.append(term)
    return terms


def send(is_odd, y, parts, a, top, odd_ref, even_ref, term_ref):
    rows = y[0].shape[0]
    term_up = product(parts[-1], top, ((1,), (0,)))
    term_ref[...] = term_up
    up = (term_up, product(split(a[-1]), top, ((1,), (0,))))
    down = (y[0], a[0])
    for holds, up_ref, down_ref in (
        (is_odd, odd_ref, even_ref),
        (jnp.logical_not(is_odd), even_ref, odd_ref),
    ):

        @pl.when(holds)
        def _(up_ref=up_ref, down_ref=down_ref):
            for ref, pair in ((up_ref, up), (down_ref, down)):
                ref[:rows, :] = pair[0]
                ref[rows:, :] = pair[1]


def split_kernel(d_ref, c_ref, dh, dl, ch, cl):
    for ref, high, low in ((d_ref, dh, dl), (c_ref, ch, cl)):
        for n in range(ref.shape[0]):
            high[n], low[n] = split(ref[n])


def in_rank_order(flags, count):
    return [jnp.where(flags[2] == 1, count - 1 - i, i) for i in range(count)]


def start_kernel(count, flags, got_ref, dh, dl, ch, cl, y_ref, a_ref, odd_ref, even_ref, term_ref):
    rows = got_ref.shape[0] // count
    for i, at in enumerate(in_rank_order(flags, count)):
        at = pl.multiple_of(at * rows, rows)
        y_ref[i * rows : (i + 1) * rows, :] = got_ref[pl.ds(at, rows), :]
    y = blocks_of(y_ref, dh.shape[1])
    parts = [split(block) for block in y]
    coupling = lambda n: (ch[n], cl[n])
    a = local_terms(y, parts, lambda n: (dh[n], dl[n]), coupling)
    a = [term / filter_half for term in a]
    a_ref[...] = jnp.concatenate(a, axis=1)
    send(flags[0] == 1, y, parts, a, coupling(len(y) - 1), odd_ref, even_ref, term_ref)


def step_kernel(
    scale,
    flags,
    y_ref,
    a_ref,
    got_odd,
    got_even,
    around_ref,
    got_term,
    dh,
    dl,
    ch,
    cl,
    b_ref,
    next_ref=None,
    odd_ref=None,
    even_ref=None,
    term_ref=None,
):
    size = dh.shape[1]
    double = 2.0 / filter_half
    is_odd = flags[0] == 1
    diagonal, coupling = lambda n: (dh[n], dl[n]), lambda n: (ch[n], cl[n])
    y, a = blocks_of(y_ref, size), blocks_of(a_ref, size)
    top = coupling(len(y) - 1)
    rows = y[0].shape[0]

    def above(rows_of):
        return jnp.where(is_odd, got_odd[rows_of, :], got_even[rows_of, :])

    def below(rows_of):
        return jnp.where(is_odd, got_even[rows_of, :], got_odd[rows_of, :])

    edge, part = slice(0, rows), slice(rows, 2 * rows)
    a[-1] = a[-1] + scale * product(split(above(edge)), top, ((1,), (1,)))
    a[0] = a[0] + scale * below(edge)
    above_a = jnp.where(flags[1] == 1, 0.0, above(part) + scale * got_term[...])
    below_a = below(part) + around_ref[...]
    terms = local_terms(a, [split(block) for block in a], diagonal, coupling)
    b = [double * term - old for term, old in zip(terms, y)]
    b[-1] = b[-1] + double * product(split(above_a), top, ((1,), (1,)))
    b[0] = b[0] + double * below_a
    b_ref[...] = jnp.concatenate(b, axis=1)
    if next_ref is not None:
        parts = [split(block) for block in b]
        terms = local_terms(b, parts, diagonal, coupling)
        a = [double * term - old for term, old in zip(terms, a)]
        next_ref[...] = jnp.concatenate(a, axis=1)
        send(is_odd, b, parts, a, top, odd_ref, even_ref, term_ref)


def chebyshev(y, diag_blocks, coupling, below, flags):
    places = snake()
    swaps = []
    for start in (1, 0):
        ups = [(places[i], places[i + 1]) for i in range(start, len(places) - 1, 2)]
        swaps.append(ups + [(above, below) for below, above in ups])
    rows, size = y.shape[0], diag_blocks.shape[1]
    message = jax.ShapeDtypeStruct((2 * rows, size), jnp.float32)
    panel = jax.ShapeDtypeStruct(y.shape, jnp.float32)
    sends = [panel, message, message, jax.ShapeDtypeStruct((rows, size), jnp.float32)]
    halves = [jax.ShapeDtypeStruct(diag_blocks.shape, jnp.bfloat16)] * 4
    hamiltonian = call(split_kernel, halves, (), diag_blocks, coupling)
    y, a, odd, even, term = call(
        functools.partial(start_kernel, lax.axis_size("yl")),
        [panel] + sends,
        (flags,),
        y,
        *hamiltonian,
    )
    for turn in range(0, DEGREE, 2):
        scale = (1.0 if turn == 0 else 2.0) / filter_half
        odd = lax.ppermute(odd, SUM, swaps[0])
        even = lax.ppermute(even, SUM, swaps[1])
        around = scale * dot(
            dot(y[:, :size], below, ((1,), (1,))), below, ((1,), (0,))
        )
        final = turn + 2 >= DEGREE
        result = call(
            functools.partial(step_kernel, scale),
            [panel] if final else [panel] + sends,
            (flags,),
            y,
            a,
            odd,
            even,
            around,
            term,
            *hamiltonian,
        )
        y = result[0]
        if not final:
            a, odd, even, term = result[1:]
    return y


def gram_half(own_ref, ref):
    tiles = product(split(own_ref[...]), split(ref[...]), ((1,), (1,)))
    ones = jnp.ones((TILE, own_ref.shape[1]), jnp.bfloat16)
    sums = [
        lax.dot_general(ones, part, (((1,), (1,)), ((), ())), preferred_element_type=jnp.float32)
        for part in split(ref[...] * ref[...])
    ]
    return tiles, sums[0] + sums[1]


def near_kernel(own_ref, near_ref, tiles_ref, squares_ref):
    tiles_ref[...], squares_ref[...] = gram_half(own_ref, near_ref)


def gram_kernel(own_ref, tiles_ref, squares_ref, far_ref, out_ref):
    tiles, squares = zip((tiles_ref[...], squares_ref[...]), gram_half(own_ref, far_ref))
    across = far_ref.shape[0] // LANES
    step = 2 * TILE + 1
    for m in range(out_ref.shape[0] // step):
        i, j = m // across * TILE, m % across * LANES
        for side in range(2):
            out_ref[step * m + TILE * side : step * m + TILE * (side + 1), :] = tiles[side][
                i : i + TILE, j : j + LANES
            ]
        side, j = m % (2 * across) // across, m % across * LANES
        out_ref[step * m + 2 * TILE : step * (m + 1), :] = squares[side][:1, j : j + LANES]


def sum_kernel(in_ref, out_ref):
    step = 2 * TILE + 1
    group = TILE * step
    count = in_ref.shape[0] // group
    total = in_ref[:group, :]
    for g in range(1, count):
        total = total + in_ref[group * g : group * (g + 1), :]
    out_ref[:group, :] = total
    piece = out_ref[:step, :]
    for m in range(1, TILE):
        piece = piece + out_ref[step * m : step * (m + 1), :]
    for m in range(TILE):
        out_ref[step * m : step * (m + 1), :] = piece
    total = out_ref[:group, :]
    for g in range(1, count):
        out_ref[group * g : group * (g + 1), :] = total


def mixing_kernel(total_rows, count, at_ref, flags, summed_ref, own_ref, near_ref, far_ref, out_ref):
    step = 2 * TILE + 1
    across = near_ref.shape[0] // LANES
    group = own_ref.shape[0]

    def scales_of(m):
        row = summed_ref[pl.ds(step * m + 2 * TILE, 1), :]
        return 1.0 / jnp.sqrt(row / total_rows + epsilon)

    on_diagonal = lax.broadcasted_iota(jnp.int32, (group, LANES), 0) == (
        lax.broadcasted_iota(jnp.int32, (group, LANES), 1)
    )
    mine = jnp.sum(jnp.where(on_diagonal, scales_of(at_ref[0]), 0.0), axis=1, keepdims=True)
    result = 1.5 * mine * own_ref[...]
    for side, ref in enumerate((near_ref, far_ref)):
        columns = []
        for j in range(across):
            column = jnp.concatenate(
                [
                    summed_ref[step * m + TILE * side : step * m + TILE * (side + 1), :]
                    for m in range(j, group // TILE * across, across)
                ]
            )
            scale = scales_of(side * across + j)
            columns.append((0.5 / total_rows) * (column * mine * scale) * scale)
        mixing = jnp.concatenate(columns, axis=1)
        result = result - product(split(mixing), split(ref[...]), ((1,), (0,)))
    rows = group // count
    for i, to in enumerate(in_rank_order(flags, count)):
        to = pl.multiple_of(to * rows, rows)
        out_ref[pl.ds(to, rows), :] = result[i * rows : (i + 1) * rows, :]


def call(kernel, out_shapes, scalars, *arrays):
    vmem = pl.BlockSpec(memory_space=pltpu.VMEM)
    smem = pl.BlockSpec(memory_space=pltpu.SMEM)
    return pl.pallas_call(
        kernel,
        out_shape=out_shapes,
        in_specs=[smem] * len(scalars) + [vmem] * len(arrays),
        out_specs=[vmem] * len(out_shapes),
        compiler_params=pltpu.CompilerParams(vmem_limit_bytes=24 * 2**20),
        interpret=INTERPRET,
    )(*scalars, *arrays)


def local(diag_blocks, coupling, vectors):
    count, width = vectors.shape
    blocks = diag_blocks.shape[0]
    nyl, nx, _ = (lax.axis_size(a) for a in VEC)
    total_rows = width * lax.axis_size(ROW)
    at, vectors = lax.optimization_barrier((lax.axis_index("x").reshape(1), vectors))
    flip = flipped(lax.axis_index("yh"), lax.axis_index("z"))
    places = snake()
    groups = [places[i : i + nyl] for i in range(0, len(places), nyl)]

    def exchange_chunks(a):
        return lax.all_to_all(
            a, SUM, split_axis=0, concat_axis=0, axis_index_groups=groups, tiled=True
        )

    yl = lax.axis_index("yl")
    chunk = jnp.where(flip, nyl - 1 - yl, yl)
    part, group, depth = blocks // nyl, nyl * count, width // nyl
    chunks = vectors.reshape(count, nyl, depth).transpose(1, 0, 2)
    own = exchange_chunks(chunks)
    own = own.reshape(group, depth)
    is_top = (lax.axis_index(ROW) == lax.axis_size(ROW) - 1) & (chunk == nyl - 1)
    own_diag = lax.dynamic_slice_in_dim(diag_blocks, chunk * part, part)
    own_coupling = lax.dynamic_slice_in_dim(coupling, chunk * part, part)
    flags = jnp.stack([chunk % 2, is_top.astype(jnp.int32), flip.astype(jnp.int32)])
    own = chebyshev(
        own,
        own_diag,
        own_coupling,
        edge_coupling(coupling, chunk),
        flags,
    )
    copies = jnp.broadcast_to(own[None], (nx, group, depth))
    near = lax.all_to_all(copies, "x", split_axis=0, concat_axis=0, tiled=True)
    near = near.reshape(nx * group, depth)
    far = lax.ppermute(near, "c", [(0, 1), (1, 0)])
    half_types = [jax.ShapeDtypeStruct((n, nx * group), jnp.float32) for n in (group, TILE)]
    halves = call(near_kernel, half_types, (), own, near)
    members = group // TILE * nx
    packed = (members * (2 * TILE + 1), LANES)
    packed_type = jax.ShapeDtypeStruct(packed, jnp.float32)

    def exchange(a):
        a = a.reshape(lax.axis_size(SUM), -1)
        return lax.all_to_all(a, SUM, split_axis=0, concat_axis=0, tiled=True).reshape(packed)

    pieces = exchange(call(gram_kernel, [packed_type], (), own, *halves, far)[0])
    summed = exchange(call(sum_kernel, [packed_type], (), pieces)[0])
    renewed = call(
        functools.partial(mixing_kernel, total_rows, nyl),
        [jax.ShapeDtypeStruct((group, depth), jnp.float32)],
        (at, flags),
        summed,
        own,
        near,
        far,
    )[0]
    back = renewed.reshape(nyl, count, depth)
    back = exchange_chunks(back)
    return back.transpose(1, 0, 2).reshape(count, width)


def solution(mesh):
    sizes = tuple(size for _, size in SPLIT)
    fine = Mesh(mesh.devices.reshape(sizes), tuple(name for name, _ in SPLIT))
    placed = (P(ROW, None, None), P(ROW, None, None), P(VEC, ROW))
    return jax.shard_map(
        local, mesh=fine, in_specs=placed, out_specs=P(VEC, ROW), check_vma=False
    )
```

```python
import functools

import jax
import jax.numpy as jnp
from jax import lax
from jax.experimental import pallas as pl
from jax.experimental.pallas import tpu as pltpu
from jax.sharding import Mesh, PartitionSpec as P


DEGREE = 4

filter_center = 0.1
filter_half = 1.0
epsilon = 1e-06
precision = lax.Precision.HIGH

SPLIT = (("yl", 4), ("x", 4), ("c", 2), ("yh", 2), ("z", 8))
VEC = ("yl", "x", "c")
ROW = ("yh", "z")
SUM = ("yh", "yl", "z")
PLANE = ("yl", "yh", "z")

TILE, LANES = 8, 128
INTERPRET = False


def dot(a, b, contract, batch=((), ())):
    return lax.dot_general(a, b, (contract, batch), precision=precision)


def flipped(yh, z):
    return (yh + z) % 2 == 0


def snake():
    nyl, nyh, nz = (lax.axis_size(a) for a in PLANE)
    places = []
    for yh in range(nyh):
        for z in range(nz):
            order = range(nyl)
            for yl in reversed(order) if flipped(yh, z) else order:
                places.append((yl * nyh + yh) * nz + z)
    return places


def edge_coupling(coupling, chunk):
    places = snake()
    nyl = lax.axis_size("yl")
    crossings = [(places[i - 1], places[i]) for i in range(nyl, len(places), nyl)]
    crossed = lax.ppermute(coupling[-1], PLANE, crossings)
    part = coupling.shape[0] // nyl
    inside = lax.dynamic_index_in_dim(
        coupling, jnp.maximum(chunk * part - 1, 0), axis=0, keepdims=False
    )
    return jnp.where(chunk == 0, crossed, inside)


def split(a):
    high = a.astype(jnp.bfloat16)
    return high, (a - high.astype(jnp.float32)).astype(jnp.bfloat16)


def product(a, b, contract):
    def one(x, y):
        return lax.dot_general(x, y, (contract, ((), ())), preferred_element_type=jnp.float32)

    return one(a[0], b[0]) + (one(a[0], b[1]) + one(a[1], b[0]))


def blocks_of(ref, size):
    return [ref[:, n : n + size] for n in range(0, ref.shape[1], size)]


def local_terms(y, parts, diagonal, coupling):
    terms = []
    for n, block in enumerate(y):
        term = product(parts[n], diagonal(n), ((1,), (0,))) - filter_center * block
        if n + 1 < len(y):
            term = term + product(parts[n + 1], coupling(n), ((1,), (1,)))
        if n > 0:
            term = term + product(parts[n - 1], coupling(n - 1), ((1,), (0,)))
        terms.append(term)
    return terms


def send(is_odd, y, parts, a, top, odd_ref, even_ref, term_ref):
    rows = y[0].shape[0]
    term_up = product(parts[-1], top, ((1,), (0,)))
    term_ref[...] = term_up
    up = (term_up, product(split(a[-1]), top, ((1,), (0,))))
    down = (y[0], a[0])
    for holds, up_ref, down_ref in (
        (is_odd, odd_ref, even_ref),
        (jnp.logical_not(is_odd), even_ref, odd_ref),
    ):

        @pl.when(holds)
        def _(up_ref=up_ref, down_ref=down_ref):
            for ref, pair in ((up_ref, up), (down_ref, down)):
                ref[:rows, :] = pair[0]
                ref[rows:, :] = pair[1]


def split_kernel(d_ref, c_ref, dh, dl, ch, cl):
    for ref, high, low in ((d_ref, dh, dl), (c_ref, ch, cl)):
        for n in range(ref.shape[0]):
            high[n], low[n] = split(ref[n])


def in_rank_order(flags, count):
    return [jnp.where(flags[2] == 1, count - 1 - i, i) for i in range(count)]


def start_kernel(count, flags, got_ref, dh, dl, ch, cl, y_ref, a_ref, odd_ref, even_ref, term_ref):
    rows = got_ref.shape[0] // count
    for i, at in enumerate(in_rank_order(flags, count)):
        at = pl.multiple_of(at * rows, rows)
        y_ref[i * rows : (i + 1) * rows, :] = got_ref[pl.ds(at, rows), :]
    y = blocks_of(y_ref, dh.shape[1])
    parts = [split(block) for block in y]
    coupling = lambda n: (ch[n], cl[n])
    a = local_terms(y, parts, lambda n: (dh[n], dl[n]), coupling)
    a = [term / filter_half for term in a]
    a_ref[...] = jnp.concatenate(a, axis=1)
    send(flags[0] == 1, y, parts, a, coupling(len(y) - 1), odd_ref, even_ref, term_ref)


def step_kernel(
    scale,
    flags,
    y_ref,
    a_ref,
    got_odd,
    got_even,
    around_ref,
    got_term,
    dh,
    dl,
    ch,
    cl,
    b_ref,
    next_ref=None,
    odd_ref=None,
    even_ref=None,
    term_ref=None,
):
    size = dh.shape[1]
    double = 2.0 / filter_half
    is_odd = flags[0] == 1
    diagonal, coupling = lambda n: (dh[n], dl[n]), lambda n: (ch[n], cl[n])
    y, a = blocks_of(y_ref, size), blocks_of(a_ref, size)
    top = coupling(len(y) - 1)
    rows = y[0].shape[0]

    def above(rows_of):
        return jnp.where(is_odd, got_odd[rows_of, :], got_even[rows_of, :])

    def below(rows_of):
        return jnp.where(is_odd, got_even[rows_of, :], got_odd[rows_of, :])

    edge, part = slice(0, rows), slice(rows, 2 * rows)
    a[-1] = a[-1] + scale * product(split(above(edge)), top, ((1,), (1,)))
    a[0] = a[0] + scale * below(edge)
    above_a = jnp.where(flags[1] == 1, 0.0, above(part) + scale * got_term[...])
    below_a = below(part) + around_ref[...]
    terms = local_terms(a, [split(block) for block in a], diagonal, coupling)
    b = [double * term - old for term, old in zip(terms, y)]
    b[-1] = b[-1] + double * product(split(above_a), top, ((1,), (1,)))
    b[0] = b[0] + double * below_a
    b_ref[...] = jnp.concatenate(b, axis=1)
    if next_ref is not None:
        parts = [split(block) for block in b]
        terms = local_terms(b, parts, diagonal, coupling)
        a = [double * term - old for term, old in zip(terms, a)]
        next_ref[...] = jnp.concatenate(a, axis=1)
        send(is_odd, b, parts, a, top, odd_ref, even_ref, term_ref)


def chebyshev(y, diag_blocks, coupling, below, flags):
    places = snake()
    swaps = []
    for start in (1, 0):
        ups = [(places[i], places[i + 1]) for i in range(start, len(places) - 1, 2)]
        swaps.append(ups + [(above, below) for below, above in ups])
    rows, size = y.shape[0], diag_blocks.shape[1]
    message = jax.ShapeDtypeStruct((2 * rows, size), jnp.float32)
    panel = jax.ShapeDtypeStruct(y.shape, jnp.float32)
    sends = [panel, message, message, jax.ShapeDtypeStruct((rows, size), jnp.float32)]
    halves = [jax.ShapeDtypeStruct(diag_blocks.shape, jnp.bfloat16)] * 4
    hamiltonian = call(split_kernel, halves, (), diag_blocks, coupling)
    y, a, odd, even, term = call(
        functools.partial(start_kernel, lax.axis_size("yl")),
        [panel] + sends,
        (flags,),
        y,
        *hamiltonian,
    )
    for turn in range(0, DEGREE, 2):
        scale = (1.0 if turn == 0 else 2.0) / filter_half
        odd = lax.ppermute(odd, PLANE, swaps[0])
        even = lax.ppermute(even, PLANE, swaps[1])
        around = scale * dot(
            dot(y[:, :size], below, ((1,), (1,))), below, ((1,), (0,))
        )
        final = turn + 2 >= DEGREE
        result = call(
            functools.partial(step_kernel, scale),
            [panel] if final else [panel] + sends,
            (flags,),
            y,
            a,
            odd,
            even,
            around,
            term,
            *hamiltonian,
        )
        y = result[0]
        if not final:
            a, odd, even, term = result[1:]
    return y


def gram_half(own_ref, ref):
    tiles = product(split(own_ref[...]), split(ref[...]), ((1,), (1,)))
    ones = jnp.ones((TILE, own_ref.shape[1]), jnp.bfloat16)
    sums = [
        lax.dot_general(ones, part, (((1,), (1,)), ((), ())), preferred_element_type=jnp.float32)
        for part in split(ref[...] * ref[...])
    ]
    return tiles, sums[0] + sums[1]


def near_kernel(own_ref, near_ref, tiles_ref, squares_ref):
    tiles_ref[...], squares_ref[...] = gram_half(own_ref, near_ref)


def gram_kernel(own_ref, tiles_ref, squares_ref, far_ref, out_ref):
    tiles, squares = zip((tiles_ref[...], squares_ref[...]), gram_half(own_ref, far_ref))
    across = far_ref.shape[0] // LANES
    step = 2 * TILE + 1
    for m in range(out_ref.shape[0] // step):
        i, j = m // across * TILE, m % across * LANES
        for side in range(2):
            out_ref[step * m + TILE * side : step * m + TILE * (side + 1), :] = tiles[side][
                i : i + TILE, j : j + LANES
            ]
        side, j = m % (2 * across) // across, m % across * LANES
        out_ref[step * m + 2 * TILE : step * (m + 1), :] = squares[side][:1, j : j + LANES]


def sum_kernel(in_ref, out_ref):
    step = 2 * TILE + 1
    group = TILE * step
    count = in_ref.shape[0] // group
    total = in_ref[:group, :]
    for g in range(1, count):
        total = total + in_ref[group * g : group * (g + 1), :]
    out_ref[:group, :] = total
    piece = out_ref[:step, :]
    for m in range(1, TILE):
        piece = piece + out_ref[step * m : step * (m + 1), :]
    for m in range(TILE):
        out_ref[step * m : step * (m + 1), :] = piece
    total = out_ref[:group, :]
    for g in range(1, count):
        out_ref[group * g : group * (g + 1), :] = total


def mixing_kernel(total_rows, count, at_ref, flags, summed_ref, own_ref, near_ref, far_ref, out_ref):
    step = 2 * TILE + 1
    across = near_ref.shape[0] // LANES
    group = own_ref.shape[0]

    def scales_of(m):
        row = summed_ref[pl.ds(step * m + 2 * TILE, 1), :]
        return 1.0 / jnp.sqrt(row / total_rows + epsilon)

    on_diagonal = lax.broadcasted_iota(jnp.int32, (group, LANES), 0) == (
        lax.broadcasted_iota(jnp.int32, (group, LANES), 1)
    )
    mine = jnp.sum(jnp.where(on_diagonal, scales_of(at_ref[0]), 0.0), axis=1, keepdims=True)
    result = 1.5 * mine * own_ref[...]
    for side, ref in enumerate((near_ref, far_ref)):
        columns = []
        for j in range(across):
            column = jnp.concatenate(
                [
                    summed_ref[step * m + TILE * side : step * m + TILE * (side + 1), :]
                    for m in range(j, group // TILE * across, across)
                ]
            )
            scale = scales_of(side * across + j)
            columns.append((0.5 / total_rows) * (column * mine * scale) * scale)
        mixing = jnp.concatenate(columns, axis=1)
        result = result - product(split(mixing), split(ref[...]), ((1,), (0,)))
    rows = group // count
    reverse = flags[2] == 1
    for holds, order in (
        (reverse, range(count - 1, -1, -1)),
        (jnp.logical_not(reverse), range(count)),
    ):

        @pl.when(holds)
        def _(order=order):
            for i, to in enumerate(order):
                out_ref[to * rows : (to + 1) * rows, :] = result[i * rows : (i + 1) * rows, :]


def call(kernel, out_shapes, scalars, *arrays):
    vmem = pl.BlockSpec(memory_space=pltpu.VMEM)
    smem = pl.BlockSpec(memory_space=pltpu.SMEM)
    return pl.pallas_call(
        kernel,
        out_shape=out_shapes,
        in_specs=[smem] * len(scalars) + [vmem] * len(arrays),
        out_specs=[vmem] * len(out_shapes),
        compiler_params=pltpu.CompilerParams(vmem_limit_bytes=24 * 2**20),
        interpret=INTERPRET,
    )(*scalars, *arrays)


def local(diag_blocks, coupling, vectors):
    count, width = vectors.shape
    blocks = diag_blocks.shape[0]
    nyl, nx, _ = (lax.axis_size(a) for a in VEC)
    total_rows = width * lax.axis_size(ROW)
    at, vectors = lax.optimization_barrier((lax.axis_index("x").reshape(1), vectors))
    flip = flipped(lax.axis_index("yh"), lax.axis_index("z"))
    places = snake()
    groups = [places[i : i + nyl] for i in range(0, len(places), nyl)]

    def exchange_chunks(a):
        return lax.all_to_all(
            a, PLANE, split_axis=0, concat_axis=0, axis_index_groups=groups, tiled=True
        )

    yl = lax.axis_index("yl")
    chunk = jnp.where(flip, nyl - 1 - yl, yl)
    part, group, depth = blocks // nyl, nyl * count, width // nyl
    chunks = vectors.reshape(count, nyl, depth).transpose(1, 0, 2)
    own = exchange_chunks(chunks)
    own = own.reshape(group, depth)
    is_top = (lax.axis_index(ROW) == lax.axis_size(ROW) - 1) & (chunk == nyl - 1)
    own_diag = lax.dynamic_slice_in_dim(diag_blocks, chunk * part, part)
    own_coupling = lax.dynamic_slice_in_dim(coupling, chunk * part, part)
    flags = jnp.stack([chunk % 2, is_top.astype(jnp.int32), flip.astype(jnp.int32)])
    own = chebyshev(
        own,
        own_diag,
        own_coupling,
        edge_coupling(coupling, chunk),
        flags,
    )
    copies = jnp.broadcast_to(own[None], (nx, group, depth))
    near = lax.all_to_all(copies, "x", split_axis=0, concat_axis=0, tiled=True)
    near = near.reshape(nx * group, depth)
    far = lax.ppermute(near, "c", [(0, 1), (1, 0)])
    half_types = [jax.ShapeDtypeStruct((n, nx * group), jnp.float32) for n in (group, TILE)]
    halves = call(near_kernel, half_types, (), own, near)
    members = group // TILE * nx
    packed = (members * (2 * TILE + 1), LANES)
    packed_type = jax.ShapeDtypeStruct(packed, jnp.float32)

    def exchange(a):
        a = a.reshape(lax.axis_size(SUM), -1)
        return lax.all_to_all(a, SUM, split_axis=0, concat_axis=0, tiled=True).reshape(packed)

    pieces = exchange(call(gram_kernel, [packed_type], (), own, *halves, far)[0])
    summed = exchange(call(sum_kernel, [packed_type], (), pieces)[0])
    renewed = call(
        functools.partial(mixing_kernel, total_rows, nyl),
        [jax.ShapeDtypeStruct((group, depth), jnp.float32)],
        (at, flags),
        summed,
        own,
        near,
        far,
    )[0]
    back = renewed.reshape(nyl, count, depth)
    back = exchange_chunks(back)
    return back.transpose(1, 0, 2).reshape(count, width)


def solution(mesh):
    sizes = tuple(size for _, size in SPLIT)
    fine = Mesh(mesh.devices.reshape(sizes), tuple(name for name, _ in SPLIT))
    placed = (P(ROW, None, None), P(ROW, None, None), P(VEC, ROW))
    return jax.shard_map(
        local, mesh=fine, in_specs=placed, out_specs=P(VEC, ROW), check_vma=False
    )
```

```python
import functools

import jax
import jax.numpy as jnp
from jax import lax
from jax.experimental import pallas as pl
from jax.experimental.pallas import tpu as pltpu
from jax.sharding import Mesh, PartitionSpec as P


DEGREE = 4

filter_center = 0.1
filter_half = 1.0
epsilon = 1e-06
precision = lax.Precision.HIGH

SPLIT = (("yl", 4), ("x", 4), ("c", 2), ("yh", 2), ("z", 8))
VEC = ("yl", "x", "c")
ROW = ("yh", "z")
SUM = ("yh", "yl", "z")
PLANE = ("yl", "yh", "z")

TILE, LANES = 8, 128
INTERPRET = False


def dot(a, b, contract, batch=((), ())):
    return lax.dot_general(a, b, (contract, batch), precision=precision)


def flipped(yh, z):
    return (yh + z) % 2 == 0


def snake():
    nyl, nyh, nz = (lax.axis_size(a) for a in PLANE)
    places = []
    for yh in range(nyh):
        for z in range(nz):
            order = range(nyl)
            for yl in reversed(order) if flipped(yh, z) else order:
                places.append((yl * nyh + yh) * nz + z)
    return places


def edge_coupling(coupling, chunk):
    places = snake()
    nyl = lax.axis_size("yl")
    crossings = [(places[i - 1], places[i]) for i in range(nyl, len(places), nyl)]
    crossed = lax.ppermute(coupling[-1], PLANE, crossings)
    part = coupling.shape[0] // nyl
    inside = lax.dynamic_index_in_dim(
        coupling, jnp.maximum(chunk * part - 1, 0), axis=0, keepdims=False
    )
    return jnp.where(chunk == 0, crossed, inside)


def split(a):
    high = a.astype(jnp.bfloat16)
    return high, (a - high.astype(jnp.float32)).astype(jnp.bfloat16)


def product(a, b, contract):
    def one(x, y):
        return lax.dot_general(x, y, (contract, ((), ())), preferred_element_type=jnp.float32)

    rows = a[0].shape[0]
    both = one(jnp.concatenate(a), b[0])
    return both[:rows] + (both[rows:] + one(a[0], b[1]))


def blocks_of(ref, size):
    return [ref[:, n : n + size] for n in range(0, ref.shape[1], size)]


def local_terms(y, parts, diagonal, coupling):
    terms = []
    for n, block in enumerate(y):
        term = product(parts[n], diagonal(n), ((1,), (0,))) - filter_center * block
        if n + 1 < len(y):
            term = term + product(parts[n + 1], coupling(n), ((1,), (1,)))
        if n > 0:
            term = term + product(parts[n - 1], coupling(n - 1), ((1,), (0,)))
        terms.append(term)
    return terms


def send(is_odd, y, parts, a, top, odd_ref, even_ref, term_ref):
    rows = y[0].shape[0]
    term_up = product(parts[-1], top, ((1,), (0,)))
    term_ref[...] = term_up
    up = (term_up, product(split(a[-1]), top, ((1,), (0,))))
    down = (y[0], a[0])
    for holds, up_ref, down_ref in (
        (is_odd, odd_ref, even_ref),
        (jnp.logical_not(is_odd), even_ref, odd_ref),
    ):

        @pl.when(holds)
        def _(up_ref=up_ref, down_ref=down_ref):
            for ref, pair in ((up_ref, up), (down_ref, down)):
                ref[:rows, :] = pair[0]
                ref[rows:, :] = pair[1]


def start_kernel(flags, y_ref, d_ref, c_ref, dh, dl, ch, cl, a_ref, odd_ref, even_ref, term_ref):
    for ref, high, low in ((d_ref, dh, dl), (c_ref, ch, cl)):
        for n in range(ref.shape[0]):
            high[n], low[n] = split(ref[n])
    size = d_ref.shape[1]
    y = blocks_of(y_ref, size)
    parts = [split(block) for block in y]
    coupling = lambda n: (ch[n], cl[n])
    a = local_terms(y, parts, lambda n: (dh[n], dl[n]), coupling)
    a = [term / filter_half for term in a]
    a_ref[...] = jnp.concatenate(a, axis=1)
    send(flags[0] == 1, y, parts, a, coupling(len(y) - 1), odd_ref, even_ref, term_ref)


def step_kernel(
    scale,
    flags,
    y_ref,
    a_ref,
    got_odd,
    got_even,
    around_ref,
    got_term,
    dh,
    dl,
    ch,
    cl,
    b_ref,
    next_ref=None,
    odd_ref=None,
    even_ref=None,
    term_ref=None,
):
    size = dh.shape[1]
    double = 2.0 / filter_half
    is_odd = flags[0] == 1
    diagonal, coupling = lambda n: (dh[n], dl[n]), lambda n: (ch[n], cl[n])
    y, a = blocks_of(y_ref, size), blocks_of(a_ref, size)
    top = coupling(len(y) - 1)
    rows = y[0].shape[0]

    def above(rows_of):
        return jnp.where(is_odd, got_odd[rows_of, :], got_even[rows_of, :])

    def below(rows_of):
        return jnp.where(is_odd, got_even[rows_of, :], got_odd[rows_of, :])

    edge, part = slice(0, rows), slice(rows, 2 * rows)
    a[-1] = a[-1] + scale * product(split(above(edge)), top, ((1,), (1,)))
    a[0] = a[0] + scale * below(edge)
    above_a = jnp.where(flags[1] == 1, 0.0, above(part) + scale * got_term[...])
    below_a = below(part) + around_ref[...]
    terms = local_terms(a, [split(block) for block in a], diagonal, coupling)
    b = [double * term - old for term, old in zip(terms, y)]
    b[-1] = b[-1] + double * product(split(above_a), top, ((1,), (1,)))
    b[0] = b[0] + double * below_a
    b_ref[...] = jnp.concatenate(b, axis=1)
    if next_ref is not None:
        parts = [split(block) for block in b]
        terms = local_terms(b, parts, diagonal, coupling)
        a = [double * term - old for term, old in zip(terms, a)]
        next_ref[...] = jnp.concatenate(a, axis=1)
        send(is_odd, b, parts, a, top, odd_ref, even_ref, term_ref)


def chebyshev(y, diag_blocks, coupling, below, flags):
    places = snake()
    swaps = []
    for start in (1, 0):
        ups = [(places[i], places[i + 1]) for i in range(start, len(places) - 1, 2)]
        swaps.append(ups + [(above, below) for below, above in ups])
    rows, size = y.shape[0], diag_blocks.shape[1]
    message = jax.ShapeDtypeStruct((2 * rows, size), jnp.float32)
    panel = jax.ShapeDtypeStruct(y.shape, jnp.float32)
    sends = [panel, message, message, jax.ShapeDtypeStruct((rows, size), jnp.float32)]
    halves = [jax.ShapeDtypeStruct(diag_blocks.shape, jnp.bfloat16)] * 4
    *hamiltonian, a, odd, even, term = call(
        start_kernel, halves + sends, (flags,), y, diag_blocks, coupling
    )
    for turn in range(0, DEGREE, 2):
        scale = (1.0 if turn == 0 else 2.0) / filter_half
        odd = lax.ppermute(odd, PLANE, swaps[0])
        even = lax.ppermute(even, PLANE, swaps[1])
        around = scale * dot(
            dot(y[:, :size], below, ((1,), (1,))), below, ((1,), (0,))
        )
        final = turn + 2 >= DEGREE
        result = call(
            functools.partial(step_kernel, scale),
            [panel] if final else [panel] + sends,
            (flags,),
            y,
            a,
            odd,
            even,
            around,
            term,
            *hamiltonian,
        )
        y = result[0]
        if not final:
            a, odd, even, term = result[1:]
    return y


def spread_kernel(flip, in_ref, out_ref, sems):
    count, _, depth = out_ref.shape
    copies = []
    for j in range(count):
        at = jnp.where(flip[0] == 1, count - 1 - j, j) * depth
        source = in_ref.at[:, pl.ds(pl.multiple_of(at, depth), depth)]
        copies.append(pltpu.make_async_copy(source, out_ref.at[j], sems.at[j]))
    for copy in copies:
        copy.start()
    for copy in copies:
        copy.wait()


def spread(flip, vectors, count):
    rows, width = vectors.shape
    return pl.pallas_call(
        spread_kernel,
        out_shape=jax.ShapeDtypeStruct((count, rows, width // count), jnp.float32),
        in_specs=[
            pl.BlockSpec(memory_space=pltpu.SMEM),
            pl.BlockSpec(memory_space=pltpu.HBM),
        ],
        out_specs=pl.BlockSpec(memory_space=pltpu.VMEM),
        scratch_shapes=[pltpu.SemaphoreType.DMA((count,))],
        name="spread",
        compiler_params=pltpu.CompilerParams(vmem_limit_bytes=24 * 2**20),
        interpret=INTERPRET,
    )(flip, vectors)


def gram_half(own_ref, ref):
    tiles = product(split(own_ref[...]), split(ref[...]), ((1,), (1,)))
    ones = jnp.ones((TILE, own_ref.shape[1]), jnp.bfloat16)
    sums = [
        lax.dot_general(ones, part, (((1,), (1,)), ((), ())), preferred_element_type=jnp.float32)
        for part in split(ref[...] * ref[...])
    ]
    return tiles, sums[0] + sums[1]


def near_kernel(own_ref, near_ref, tiles_ref, squares_ref):
    tiles_ref[...], squares_ref[...] = gram_half(own_ref, near_ref)


def gram_kernel(own_ref, tiles_ref, squares_ref, far_ref, out_ref):
    tiles, squares = zip((tiles_ref[...], squares_ref[...]), gram_half(own_ref, far_ref))
    across = far_ref.shape[0] // LANES
    step = 2 * TILE + 1
    for m in range(out_ref.shape[0] // step):
        i, j = m // across * TILE, m % across * LANES
        for side in range(2):
            out_ref[step * m + TILE * side : step * m + TILE * (side + 1), :] = tiles[side][
                i : i + TILE, j : j + LANES
            ]
        side, j = m % (2 * across) // across, m % across * LANES
        out_ref[step * m + 2 * TILE : step * (m + 1), :] = squares[side][:1, j : j + LANES]


def sum_kernel(in_ref, out_ref):
    step = 2 * TILE + 1
    group = TILE * step
    count = in_ref.shape[0] // group
    total = in_ref[:group, :]
    for g in range(1, count):
        total = total + in_ref[group * g : group * (g + 1), :]
    out_ref[:group, :] = total
    piece = out_ref[:step, :]
    for m in range(1, TILE):
        piece = piece + out_ref[step * m : step * (m + 1), :]
    for m in range(TILE):
        out_ref[step * m : step * (m + 1), :] = piece
    total = out_ref[:group, :]
    for g in range(1, count):
        out_ref[group * g : group * (g + 1), :] = total


def mixing_kernel(total_rows, at_ref, summed_ref, own_ref, near_ref, far_ref, out_ref):
    step = 2 * TILE + 1
    across = near_ref.shape[0] // LANES
    group = own_ref.shape[0]

    def scales_of(m):
        row = summed_ref[pl.ds(step * m + 2 * TILE, 1), :]
        return 1.0 / jnp.sqrt(row / total_rows + epsilon)

    on_diagonal = lax.broadcasted_iota(jnp.int32, (group, LANES), 0) == (
        lax.broadcasted_iota(jnp.int32, (group, LANES), 1)
    )
    mine = jnp.sum(jnp.where(on_diagonal, scales_of(at_ref[0]), 0.0), axis=1, keepdims=True)
    result = 1.5 * mine * own_ref[...]
    for side, ref in enumerate((near_ref, far_ref)):
        columns = []
        for j in range(across):
            column = jnp.concatenate(
                [
                    summed_ref[step * m + TILE * side : step * m + TILE * (side + 1), :]
                    for m in range(j, group // TILE * across, across)
                ]
            )
            scale = scales_of(side * across + j)
            columns.append((0.5 / total_rows) * (column * mine * scale) * scale)
        mixing = jnp.concatenate(columns, axis=1)
        result = result - product(split(mixing), split(ref[...]), ((1,), (0,)))
    out_ref[...] = result


def call(kernel, out_shapes, scalars, *arrays):
    vmem = pl.BlockSpec(memory_space=pltpu.VMEM)
    smem = pl.BlockSpec(memory_space=pltpu.SMEM)
    return pl.pallas_call(
        kernel,
        out_shape=out_shapes,
        in_specs=[smem] * len(scalars) + [vmem] * len(arrays),
        out_specs=[vmem] * len(out_shapes),
        compiler_params=pltpu.CompilerParams(vmem_limit_bytes=24 * 2**20),
        interpret=INTERPRET,
    )(*scalars, *arrays)


def local(diag_blocks, coupling, vectors):
    count, width = vectors.shape
    blocks = diag_blocks.shape[0]
    nyl, nx, _ = (lax.axis_size(a) for a in VEC)
    total_rows = width * lax.axis_size(ROW)
    at, vectors = lax.optimization_barrier((lax.axis_index("x").reshape(1), vectors))
    flip = flipped(lax.axis_index("yh"), lax.axis_index("z"))
    yl = lax.axis_index("yl")
    chunk = jnp.where(flip, nyl - 1 - yl, yl)
    part, group, depth = blocks // nyl, nyl * count, width // nyl
    chunks = spread(flip.astype(jnp.int32).reshape(1), vectors, nyl)
    own = lax.all_to_all(chunks, "yl", split_axis=0, concat_axis=0, tiled=True)
    own = own.reshape(group, depth)
    is_top = (lax.axis_index(ROW) == lax.axis_size(ROW) - 1) & (chunk == nyl - 1)
    own_diag = lax.dynamic_slice_in_dim(diag_blocks, chunk * part, part)
    own_coupling = lax.dynamic_slice_in_dim(coupling, chunk * part, part)
    own = chebyshev(
        own,
        own_diag,
        own_coupling,
        edge_coupling(coupling, chunk),
        jnp.stack([chunk % 2, is_top.astype(jnp.int32)]),
    )
    copies = jnp.broadcast_to(own[None], (nx, group, depth))
    near = lax.all_to_all(copies, "x", split_axis=0, concat_axis=0, tiled=True)
    near = near.reshape(nx * group, depth)
    far = lax.ppermute(near, "c", [(0, 1), (1, 0)])
    half_types = [jax.ShapeDtypeStruct((n, nx * group), jnp.float32) for n in (group, TILE)]
    halves = call(near_kernel, half_types, (), own, near)
    members = group // TILE * nx
    packed = (members * (2 * TILE + 1), LANES)
    packed_type = jax.ShapeDtypeStruct(packed, jnp.float32)

    def exchange(a):
        a = a.reshape(lax.axis_size(SUM), -1)
        return lax.all_to_all(a, SUM, split_axis=0, concat_axis=0, tiled=True).reshape(packed)

    pieces = exchange(call(gram_kernel, [packed_type], (), own, *halves, far)[0])
    summed = exchange(call(sum_kernel, [packed_type], (), pieces)[0])
    renewed = call(
        functools.partial(mixing_kernel, total_rows),
        [jax.ShapeDtypeStruct((group, depth), jnp.float32)],
        (at,),
        summed,
        own,
        near,
        far,
    )[0]
    back = renewed.reshape(nyl, count, depth)
    back = lax.all_to_all(back, "yl", split_axis=0, concat_axis=0, tiled=True)
    back = jnp.where(flip, back[::-1], back)
    return back.transpose(1, 0, 2).reshape(count, width)


def solution(mesh):
    sizes = tuple(size for _, size in SPLIT)
    fine = Mesh(mesh.devices.reshape(sizes), tuple(name for name, _ in SPLIT))
    placed = (P(ROW, None, None), P(ROW, None, None), P(VEC, ROW))
    return jax.shard_map(
        local, mesh=fine, in_specs=placed, out_specs=P(VEC, ROW), check_vma=False
    )
```

```python
import functools

import jax
import jax.numpy as jnp
from jax import lax
from jax.experimental import pallas as pl
from jax.experimental.pallas import tpu as pltpu
from jax.sharding import Mesh, PartitionSpec as P


DEGREE = 4

filter_center = 0.1
filter_half = 1.0
epsilon = 1e-06
precision = lax.Precision.HIGH

SPLIT = (("yl", 4), ("x", 4), ("c", 2), ("yh", 2), ("z", 8))
VEC = ("yl", "x", "c")
ROW = ("yh", "z")
SUM = ("yh", "yl", "z")
PLANE = ("yl", "yh", "z")

TILE, LANES = 8, 128
INTERPRET = False


def dot(a, b, contract, batch=((), ())):
    return lax.dot_general(a, b, (contract, batch), precision=precision)


def flipped(yh, z):
    return (yh + z) % 2 == 0


def snake():
    nyl, nyh, nz = (lax.axis_size(a) for a in PLANE)
    places = []
    for yh in range(nyh):
        for z in range(nz):
            order = range(nyl)
            for yl in reversed(order) if flipped(yh, z) else order:
                places.append((yl * nyh + yh) * nz + z)
    return places


def edge_coupling(coupling, chunk):
    places = snake()
    nyl = lax.axis_size("yl")
    crossings = [(places[i - 1], places[i]) for i in range(nyl, len(places), nyl)]
    crossed = lax.ppermute(coupling[-1], PLANE, crossings)
    part = coupling.shape[0] // nyl
    inside = lax.dynamic_index_in_dim(
        coupling, jnp.maximum(chunk * part - 1, 0), axis=0, keepdims=False
    )
    return jnp.where(chunk == 0, crossed, inside)


def split(a):
    high = a.astype(jnp.bfloat16)
    return high, (a - high.astype(jnp.float32)).astype(jnp.bfloat16)


def product(a, b, contract):
    def one(x, y):
        return lax.dot_general(x, y, (contract, ((), ())), preferred_element_type=jnp.float32)

    rows = a[0].shape[0]
    both = one(jnp.concatenate(a), b[0])
    return both[:rows] + (both[rows:] + one(a[0], b[1]))


def blocks_of(ref, size):
    return [ref[:, n : n + size] for n in range(0, ref.shape[1], size)]


def local_terms(y, parts, diagonal, coupling):
    terms = []
    for n, block in enumerate(y):
        term = product(parts[n], diagonal(n), ((1,), (0,))) - filter_center * block
        if n + 1 < len(y):
            term = term + product(parts[n + 1], coupling(n), ((1,), (1,)))
        if n > 0:
            term = term + product(parts[n - 1], coupling(n - 1), ((1,), (0,)))
        terms.append(term)
    return terms


def send(is_odd, y, parts, a, top, odd_ref, even_ref, term_ref):
    rows = y[0].shape[0]
    term_up = product(parts[-1], top, ((1,), (0,)))
    term_ref[...] = term_up
    up = (term_up, product(split(a[-1]), top, ((1,), (0,))))
    down = (y[0], a[0])
    for holds, up_ref, down_ref in (
        (is_odd, odd_ref, even_ref),
        (jnp.logical_not(is_odd), even_ref, odd_ref),
    ):

        @pl.when(holds)
        def _(up_ref=up_ref, down_ref=down_ref):
            for ref, pair in ((up_ref, up), (down_ref, down)):
                ref[:rows, :] = pair[0]
                ref[rows:, :] = pair[1]


def start_kernel(flags, y_ref, d_ref, c_ref, dh, dl, ch, cl, a_ref, odd_ref, even_ref, term_ref):
    for ref, high, low in ((d_ref, dh, dl), (c_ref, ch, cl)):
        for n in range(ref.shape[0]):
            high[n], low[n] = split(ref[n])
    size = d_ref.shape[1]
    y = blocks_of(y_ref, size)
    parts = [split(block) for block in y]
    coupling = lambda n: (ch[n], cl[n])
    a = local_terms(y, parts, lambda n: (dh[n], dl[n]), coupling)
    a = [term / filter_half for term in a]
    a_ref[...] = jnp.concatenate(a, axis=1)
    send(flags[0] == 1, y, parts, a, coupling(len(y) - 1), odd_ref, even_ref, term_ref)


def step_kernel(
    scale,
    flags,
    y_ref,
    a_ref,
    got_odd,
    got_even,
    around_ref,
    got_term,
    dh,
    dl,
    ch,
    cl,
    b_ref,
    next_ref=None,
    odd_ref=None,
    even_ref=None,
    term_ref=None,
):
    size = dh.shape[1]
    double = 2.0 / filter_half
    is_odd = flags[0] == 1
    diagonal, coupling = lambda n: (dh[n], dl[n]), lambda n: (ch[n], cl[n])
    y, a = blocks_of(y_ref, size), blocks_of(a_ref, size)
    top = coupling(len(y) - 1)
    rows = y[0].shape[0]

    def above(rows_of):
        return jnp.where(is_odd, got_odd[rows_of, :], got_even[rows_of, :])

    def below(rows_of):
        return jnp.where(is_odd, got_even[rows_of, :], got_odd[rows_of, :])

    edge, part = slice(0, rows), slice(rows, 2 * rows)
    a[-1] = a[-1] + scale * product(split(above(edge)), top, ((1,), (1,)))
    a[0] = a[0] + scale * below(edge)
    above_a = jnp.where(flags[1] == 1, 0.0, above(part) + scale * got_term[...])
    below_a = below(part) + around_ref[...]
    terms = local_terms(a, [split(block) for block in a], diagonal, coupling)
    b = [double * term - old for term, old in zip(terms, y)]
    b[-1] = b[-1] + double * product(split(above_a), top, ((1,), (1,)))
    b[0] = b[0] + double * below_a
    b_ref[...] = jnp.concatenate(b, axis=1)
    if odd_ref is None:
        for i in range(next_ref.shape[0]):
            next_ref[i] = jnp.concatenate(b, axis=1)
    else:
        parts = [split(block) for block in b]
        terms = local_terms(b, parts, diagonal, coupling)
        a = [double * term - old for term, old in zip(terms, a)]
        next_ref[...] = jnp.concatenate(a, axis=1)
        send(is_odd, b, parts, a, top, odd_ref, even_ref, term_ref)


def chebyshev(y, diag_blocks, coupling, below, flags):
    places = snake()
    swaps = []
    for start in (1, 0):
        ups = [(places[i], places[i + 1]) for i in range(start, len(places) - 1, 2)]
        swaps.append(ups + [(above, below) for below, above in ups])
    rows, size = y.shape[0], diag_blocks.shape[1]
    message = jax.ShapeDtypeStruct((2 * rows, size), jnp.float32)
    panel = jax.ShapeDtypeStruct(y.shape, jnp.float32)
    copies = jax.ShapeDtypeStruct((lax.axis_size("x"), *y.shape), jnp.float32)
    sends = [panel, message, message, jax.ShapeDtypeStruct((rows, size), jnp.float32)]
    halves = [jax.ShapeDtypeStruct(diag_blocks.shape, jnp.bfloat16)] * 4
    *hamiltonian, a, odd, even, term = call(
        start_kernel, halves + sends, (flags,), y, diag_blocks, coupling
    )
    for turn in range(0, DEGREE, 2):
        scale = (1.0 if turn == 0 else 2.0) / filter_half
        odd = lax.ppermute(odd, PLANE, swaps[0])
        even = lax.ppermute(even, PLANE, swaps[1])
        around = scale * dot(
            dot(y[:, :size], below, ((1,), (1,))), below, ((1,), (0,))
        )
        final = turn + 2 >= DEGREE
        result = call(
            functools.partial(step_kernel, scale),
            [panel, copies] if final else [panel] + sends,
            (flags,),
            y,
            a,
            odd,
            even,
            around,
            term,
            *hamiltonian,
        )
        y = result[0]
        if not final:
            a, odd, even, term = result[1:]
    return result


def spread_kernel(flip, in_ref, out_ref, sems):
    count, _, depth = out_ref.shape
    copies = []
    for j in range(count):
        at = jnp.where(flip[0] == 1, count - 1 - j, j) * depth
        source = in_ref.at[:, pl.ds(pl.multiple_of(at, depth), depth)]
        copies.append(pltpu.make_async_copy(source, out_ref.at[j], sems.at[j]))
    for copy in copies:
        copy.start()
    for copy in copies:
        copy.wait()


def spread(flip, vectors, count):
    rows, width = vectors.shape
    return pl.pallas_call(
        spread_kernel,
        out_shape=jax.ShapeDtypeStruct((count, rows, width // count), jnp.float32),
        in_specs=[
            pl.BlockSpec(memory_space=pltpu.SMEM),
            pl.BlockSpec(memory_space=pltpu.HBM),
        ],
        out_specs=pl.BlockSpec(memory_space=pltpu.VMEM),
        scratch_shapes=[pltpu.SemaphoreType.DMA((count,))],
        name="spread",
        compiler_params=pltpu.CompilerParams(vmem_limit_bytes=24 * 2**20),
        interpret=INTERPRET,
    )(flip, vectors)


def gram_half(own_ref, ref):
    tiles = product(split(own_ref[...]), split(ref[...]), ((1,), (1,)))
    ones = jnp.ones((TILE, own_ref.shape[1]), jnp.bfloat16)
    sums = [
        lax.dot_general(ones, part, (((1,), (1,)), ((), ())), preferred_element_type=jnp.float32)
        for part in split(ref[...] * ref[...])
    ]
    return tiles, sums[0] + sums[1]


def near_kernel(own_ref, near_ref, tiles_ref, squares_ref):
    tiles_ref[...], squares_ref[...] = gram_half(own_ref, near_ref)


def gram_kernel(own_ref, tiles_ref, squares_ref, far_ref, out_ref):
    tiles, squares = zip((tiles_ref[...], squares_ref[...]), gram_half(own_ref, far_ref))
    across = far_ref.shape[0] // LANES
    step = 2 * TILE + 1
    for m in range(out_ref.shape[0] // step):
        i, j = m // across * TILE, m % across * LANES
        for side in range(2):
            out_ref[step * m + TILE * side : step * m + TILE * (side + 1), :] = tiles[side][
                i : i + TILE, j : j + LANES
            ]
        side, j = m % (2 * across) // across, m % across * LANES
        out_ref[step * m + 2 * TILE : step * (m + 1), :] = squares[side][:1, j : j + LANES]


def sum_kernel(in_ref, out_ref):
    step = 2 * TILE + 1
    group = TILE * step
    count = in_ref.shape[0] // group
    total = in_ref[:group, :]
    for g in range(1, count):
        total = total + in_ref[group * g : group * (g + 1), :]
    out_ref[:group, :] = total
    piece = out_ref[:step, :]
    for m in range(1, TILE):
        piece = piece + out_ref[step * m : step * (m + 1), :]
    for m in range(TILE):
        out_ref[step * m : step * (m + 1), :] = piece
    total = out_ref[:group, :]
    for g in range(1, count):
        out_ref[group * g : group * (g + 1), :] = total


def mixing_kernel(total_rows, at_ref, summed_ref, own_ref, near_ref, far_ref, out_ref):
    step = 2 * TILE + 1
    across = near_ref.shape[0] // LANES
    group = own_ref.shape[0]

    def scales_of(m):
        row = summed_ref[pl.ds(step * m + 2 * TILE, 1), :]
        return 1.0 / jnp.sqrt(row / total_rows + epsilon)

    on_diagonal = lax.broadcasted_iota(jnp.int32, (group, LANES), 0) == (
        lax.broadcasted_iota(jnp.int32, (group, LANES), 1)
    )
    mine = jnp.sum(jnp.where(on_diagonal, scales_of(at_ref[0]), 0.0), axis=1, keepdims=True)
    result = 1.5 * mine * own_ref[...]
    for side, ref in enumerate((near_ref, far_ref)):
        columns = []
        for j in range(across):
            column = jnp.concatenate(
                [
                    summed_ref[step * m + TILE * side : step * m + TILE * (side + 1), :]
                    for m in range(j, group // TILE * across, across)
                ]
            )
            scale = scales_of(side * across + j)
            columns.append((0.5 / total_rows) * (column * mine * scale) * scale)
        mixing = jnp.concatenate(columns, axis=1)
        result = result - product(split(mixing), split(ref[...]), ((1,), (0,)))
    out_ref[...] = result


def call(kernel, out_shapes, scalars, *arrays):
    vmem = pl.BlockSpec(memory_space=pltpu.VMEM)
    smem = pl.BlockSpec(memory_space=pltpu.SMEM)
    return pl.pallas_call(
        kernel,
        out_shape=out_shapes,
        in_specs=[smem] * len(scalars) + [vmem] * len(arrays),
        out_specs=[vmem] * len(out_shapes),
        compiler_params=pltpu.CompilerParams(vmem_limit_bytes=24 * 2**20),
        interpret=INTERPRET,
    )(*scalars, *arrays)


def local(diag_blocks, coupling, vectors):
    count, width = vectors.shape
    blocks = diag_blocks.shape[0]
    nyl, nx, _ = (lax.axis_size(a) for a in VEC)
    total_rows = width * lax.axis_size(ROW)
    at, vectors = lax.optimization_barrier((lax.axis_index("x").reshape(1), vectors))
    flip = flipped(lax.axis_index("yh"), lax.axis_index("z"))
    yl = lax.axis_index("yl")
    chunk = jnp.where(flip, nyl - 1 - yl, yl)
    part, group, depth = blocks // nyl, nyl * count, width // nyl
    chunks = spread(flip.astype(jnp.int32).reshape(1), vectors, nyl)
    own = lax.all_to_all(chunks, "yl", split_axis=0, concat_axis=0, tiled=True)
    own = own.reshape(group, depth)
    is_top = (lax.axis_index(ROW) == lax.axis_size(ROW) - 1) & (chunk == nyl - 1)
    own_diag = lax.dynamic_slice_in_dim(diag_blocks, chunk * part, part)
    own_coupling = lax.dynamic_slice_in_dim(coupling, chunk * part, part)
    own, copies = chebyshev(
        own,
        own_diag,
        own_coupling,
        edge_coupling(coupling, chunk),
        jnp.stack([chunk % 2, is_top.astype(jnp.int32)]),
    )
    near = lax.all_to_all(copies, "x", split_axis=0, concat_axis=0, tiled=True)
    near = near.reshape(nx * group, depth)
    far = lax.ppermute(near, "c", [(0, 1), (1, 0)])
    half_types = [jax.ShapeDtypeStruct((n, nx * group), jnp.float32) for n in (group, TILE)]
    halves = call(near_kernel, half_types, (), own, near)
    members = group // TILE * nx
    packed = (members * (2 * TILE + 1), LANES)
    packed_type = jax.ShapeDtypeStruct(packed, jnp.float32)

    def exchange(a):
        a = a.reshape(lax.axis_size(SUM), -1)
        return lax.all_to_all(a, SUM, split_axis=0, concat_axis=0, tiled=True).reshape(packed)

    pieces = exchange(call(gram_kernel, [packed_type], (), own, *halves, far)[0])
    summed = exchange(call(sum_kernel, [packed_type], (), pieces)[0])
    renewed = call(
        functools.partial(mixing_kernel, total_rows),
        [jax.ShapeDtypeStruct((group, depth), jnp.float32)],
        (at,),
        summed,
        own,
        near,
        far,
    )[0]
    back = renewed.reshape(nyl, count, depth)
    back = lax.all_to_all(back, "yl", split_axis=0, concat_axis=0, tiled=True)
    back = jnp.where(flip, back[::-1], back)
    return back.transpose(1, 0, 2).reshape(count, width)


def solution(mesh):
    sizes = tuple(size for _, size in SPLIT)
    fine = Mesh(mesh.devices.reshape(sizes), tuple(name for name, _ in SPLIT))
    placed = (P(ROW, None, None), P(ROW, None, None), P(VEC, ROW))
    return jax.shard_map(
        local, mesh=fine, in_specs=placed, out_specs=P(VEC, ROW), check_vma=False
    )
```
